256 devices in a mesh: pass: 64 (over z, y, core), voc: 4 (over x).
Axes of the slice: x: 4, y: 4, z: 8, core: 2. Of those that a mesh axis runs over, the one named last changes fastest.
Arguments:
- hidden: bfloat16 [2048, 16, 768], P('pass'), may hold values from -6 to 6
- positions: int32 [2048, 8], P('pass'), may hold values from 0 to 15
- passage_weight: float32 [2048], P('pass'), may hold values from 0.4 to 2.5
- passage_counts: int32 [128], replicated, may hold values from 1 to 24, 2048 in all
- passage_slot: int32 [2048], replicated, may hold values from 0 to 2047, each once
- head_weight: bfloat16 [768, 30720], P(None, 'voc'), may hold values from -0.21875 to 0.21875
- head_bias: float32 [30720], P('voc'), may hold values from -5 to 5
- queries: bfloat16 [128, 30720], P('pass', 'voc'), may hold values from -1 to 1
Outputs:
- scores: float32 [128, 128], P('pass')
- hidden_grad: bfloat16 [2048, 16, 768], P('pass')
The draws below stay inside these ranges and needn't reach their ends.
Inputs may be any that keep to these rules, and one draw needn't show every extreme that they name: `passage_slot`: each slot holds exactly one passage.
All inputs are finite; a program needn't handle non-finite values.
Results may differ from the reference program's by a relative error of at most 0.015.
Values may be sent and summed in bfloat16 or wider, within the bound.
A program may use at most 64 MiB of HBM per device.

```python
import math
import jax
import jax.numpy as jnp
import numpy as np
from jax import lax

D = 768
VOCAB = 30720
SEQ = 16
POS = 8
PASS_DEV = 32
DOC_DEV = 2
PASSAGES = 2048
DOCS = 128


def draw_queries(key, part):
    first = jax.random.fold_in(jax.random.fold_in(key, 17), 0)
    per_doc = max(PASS_DEV // DOC_DEV, 1) * 1.0
    spread = 2.0 / (jnp.sqrt(VOCAB * 1.0) * 2.6 * per_doc)
    base = jax.random.normal(first, (DOCS, VOCAB), jnp.float32) * spread
    return base.astype(jnp.bfloat16)


def place_ends(result, stream_key, least, top_value):
    spot = [jax.random.randint(jax.random.fold_in(stream_key, axis), (), 0, length) for axis, length in enumerate(result.shape)]
    longest = result.shape.index(max(result.shape))
    beside = spot[:longest] + [(spot[longest] + 1) % result.shape[longest]] + spot[longest + 1:]
    return result.at[tuple(spot)].set(least).at[tuple(beside)].set(top_value)


def level_of(stream_key, shape, shards, low, high):
    factor_of, own = 1.0, jax.random.fold_in(stream_key, 6)
    for axis_at, shards_of in shards:
        heights = jnp.exp(jax.random.uniform(jax.random.fold_in(own, axis_at), (shards_of,), jnp.float32, low / len(shards), high / len(shards)))
        factor_of = factor_of * jnp.repeat(heights, shape[axis_at] // shards_of).reshape([-1 if axis == axis_at else 1 for axis in range(len(shape))])
    return factor_of


def profile(amount, total, most, skew):
    weights = [(1 << 20) // math.isqrt(standing ** skew) + 1 for standing in range(2, amount + 1)]
    spare, holding = total - most - (amount - 1), [1] * (amount - 1)
    while spare > 0:
        free = [i for i in range(amount - 1) if holding[i] < most]
        mass, left = sum([weights[i] for i in free]), spare
        for i in free:
            more = min(most - holding[i], max(1, left * weights[i] // mass), spare)
            holding[i] = holding[i] + more
            spare = spare - more
    return np.array([most] + holding)


def uneven(own_key, amount, total, limit, lean):
    if amount == 2:
        one = jax.random.randint(own_key, (), max(1, total - limit), min(limit, total - 1) + 1)
        return jnp.stack([one, total - one])
    sizes = jnp.asarray(profile(amount, total, limit, lean), jnp.int32)
    pairs = (amount - 1) // 2
    source_of, receiver = sizes[1:1 + 2 * pairs:2], sizes[2:2 + 2 * pairs:2]
    slack = jnp.minimum(source_of - 1, limit - receiver)
    passed = jax.random.randint(jax.random.fold_in(own_key, 1), (pairs,), 0, 1 << 20) % (slack + 1)
    sizes = sizes.at[1:1 + 2 * pairs:2].set(source_of - passed).at[2:2 + 2 * pairs:2].set(receiver + passed)
    return sizes[jax.random.permutation(jax.random.fold_in(own_key, 2), amount)]


def gaussian(own_key, shape, scale, most, cuts=(), kind=jnp.bfloat16):
    result = scale * jax.random.normal(own_key, shape, jnp.float32)
    if cuts:
        result = result * level_of(own_key, shape, cuts, -0.22, 0.18)
    return jnp.clip(result, -most, most).astype(kind)


def setup_inputs(seed: int = 0) -> dict:
    key_list = jax.random.split(jax.random.key(seed), 9)
    hidden = gaussian(key_list[0], (PASSAGES, SEQ, D), 1.0, 6.0, ((0, 64),))
    positions = place_ends(jax.random.randint(key_list[1], (PASSAGES, POS), 0, SEQ), jax.random.fold_in(key_list[1], 1), 0, SEQ - 1).astype(jnp.int32)
    passage_weight = jnp.clip(jnp.exp(math.log(2.5) - 1.8325814 * jax.random.uniform(key_list[2], (PASSAGES,), jnp.float32) ** level_of(key_list[2], (PASSAGES,), ((0, 64),), -0.2, 0.2)), 0.4, 2.5)
    passage_counts = uneven(key_list[3], DOCS, PASSAGES, 24, 2).astype(jnp.int32)
    passage_slot = jax.random.permutation(key_list[4], PASSAGES).astype(jnp.int32)
    head_weight = gaussian(key_list[5], (D, VOCAB), D ** -0.5, 0.21875, ((1, 4),))
    head_bias = gaussian(key_list[6], (VOCAB,), 1.0, 5.0, ((0, 4),), jnp.float32)
    queries = draw_queries(jax.random.fold_in(key_list[8], 71), 0)
    return {"hidden": hidden, "positions": positions, "passage_weight": passage_weight, "passage_counts": passage_counts, "passage_slot": passage_slot, "head_weight": head_weight, "head_bias": head_bias, "queries": queries}


HIGH = lax.Precision.HIGHEST


def document_of_order(passage_counts):
    ends = jnp.cumsum(passage_counts).astype(jnp.int32)
    order = jnp.arange(PASSAGES, dtype=jnp.int32)
    return jnp.sum((ends[None, :] <= order[:, None]).astype(jnp.int32), axis=1).astype(jnp.int32)


def picked_logits(states, places, head_weight, head_bias):
    picked = jax.vmap(lambda h, p: h[p])(states, places)
    flat = picked.reshape(-1, D)
    return jnp.dot(flat, head_weight, preferred_element_type=jnp.float32) + head_bias.astype(jnp.float32)


def reference(hidden, positions, passage_weight, passage_counts, passage_slot, head_weight, head_bias, queries):
    doc_order = document_of_order(passage_counts)
    doc_slot = jnp.zeros((PASSAGES,), jnp.int32).at[passage_slot].set(doc_order)
    mixing = jnp.where(doc_slot[None, :] == jnp.arange(DOCS, dtype=jnp.int32)[:, None],
                       passage_weight[None, :].astype(jnp.float32), jnp.float32(0.0))
    blocks = PASSAGES // PASS_DEV
    hid_blocks = hidden.reshape(blocks, PASS_DEV, SEQ, D)
    pos_blocks = positions.reshape(blocks, PASS_DEV, POS)

    def forward_block(pair):
        states, places = pair
        logits = picked_logits(states, places, head_weight, head_bias)
        active = jnp.log1p(jnp.maximum(logits, 0.0))
        return active.reshape(PASS_DEV, POS, VOCAB).sum(axis=1).astype(jnp.bfloat16)

    rep = lax.map(forward_block, (hid_blocks, pos_blocks)).reshape(PASSAGES, VOCAB)
    documents = jnp.dot(mixing, rep.astype(jnp.float32), precision=HIGH)
    query_full = queries.astype(jnp.float32)
    scores = jnp.dot(query_full, documents.T, precision=HIGH)
    prob = jax.nn.softmax(scores, axis=1)
    dscore = (prob - jnp.eye(DOCS, dtype=jnp.float32)) / DOCS
    drep = jnp.dot(jnp.dot(mixing.T, dscore.T, precision=HIGH), query_full, precision=HIGH)
    drep_blocks = drep.reshape(blocks, PASS_DEV, VOCAB)

    def backward_block(triple):
        states, places, dblock = triple
        logits = picked_logits(states, places, head_weight, head_bias).reshape(PASS_DEV, POS, VOCAB)
        growth = 1.0 + jnp.maximum(logits, 0.0)
        dlogits = jnp.where(logits > 0, dblock[:, None, :] / growth, jnp.float32(0.0)).astype(jnp.bfloat16)
        dpicked = lax.dot_general(dlogits.reshape(-1, VOCAB), head_weight, (((1,), (1,)), ((), ())),
                                  preferred_element_type=jnp.float32)
        onehot = (places[:, :, None] == jnp.arange(SEQ, dtype=jnp.int32)[None, None, :]).astype(jnp.float32)
        grad = jnp.einsum('bps,bpd->bsd', onehot, dpicked.reshape(PASS_DEV, POS, D), precision=HIGH)
        return grad.astype(jnp.bfloat16)

    hidden_grad = lax.map(backward_block, (hid_blocks, pos_blocks, drep_blocks)).reshape(PASSAGES, SEQ, D)
    return scores, hidden_grad
```

```python
import functools

import jax
import jax.numpy as jnp
from jax import lax
from jax.experimental import pallas as pl
from jax.experimental.pallas import tpu as pltpu
from jax.sharding import PartitionSpec as P

MESH = pl.DeviceIdType.MESH
CORES = 2
ROWS = 4
QUARTERS = 4
FORWARD = 512
F32 = jnp.float32
BF16 = jnp.bfloat16
NT = (((1,), (1,)), ((), ()))
NN = (((1,), (0,)), ((), ()))
TN = (((0,), (0,)), ((), ()))


def dot(a, b, dims):
    return lax.dot_general(a, b, dims, preferred_element_type=F32)


def halves(a):
    high = a.astype(BF16)
    return high, (a - high.astype(F32)).astype(BF16)


def iota(shape, dim):
    return lax.broadcasted_iota(jnp.int32, shape, dim)


def kernel(
    depth,
    blocks,
    hidden,
    target,
    weights,
    counts,
    slots,
    w_hbm,
    bias,
    q_own,
    scores_out,
    grad_out,
    w,
    inv,
    rep,
    drep,
    qx,
    picked,
    onehot,
    parts,
    box_a,
    box_b,
    box_c,
    scores,
    part_own,
    part_send,
    part_box,
    total,
    w_sem,
    q_sem,
    z_send,
    z_recv,
    y_send,
    y_recv,
    c_send,
    c_recv,
    a_send,
    a_recv,
    b_send,
    b_recv,
    d_send,
    d_recv,
    e_send,
    e_recv,
    r_send,
    r_recv,
    g_send,
    g_recv,
):
    me = lax.axis_index("pass")
    x = lax.axis_index("voc")
    core = lax.rem(me, CORES)
    y = lax.rem(lax.div(me, CORES), ROWS)
    z = lax.div(me, CORES * ROWS)
    group = blocks * CORES
    g = x * CORES + core
    vocab = w.shape[1]
    width = w.shape[0]
    count = rep.shape[0]
    picks = picked.shape[0] // count
    docs_total = counts.shape[1]
    quarter = vocab // QUARTERS
    share = docs_total // group
    steps = vocab // FORWARD
    columns = width // 3
    tokens = picked.shape[0]
    piece_rows = tokens // blocks

    def place(zz, yy, cc):
        return (zz * ROWS + yy) * CORES + cc

    def z_at(k):
        return lax.rem(z + k, depth)

    def y_at(k):
        return lax.rem(y + k, ROWS)

    def x_at(k):
        return lax.rem(x + k, blocks)

    def g_at(k):
        return lax.rem(g + k, group)

    def distance(k):
        odd = lax.rem(k, 2)
        return odd * lax.div(k + 1, 2) + (1 - odd) * lax.rem(depth - lax.div(k, 2), depth)

    other = 1 - core

    def w_copy(step):
        span = pl.ds(pl.multiple_of(step * FORWARD, FORWARD), FORWARD)
        return pltpu.make_async_copy(w_hbm.at[:, span], w.at[:, span], w_sem.at[step])

    q_copy = pltpu.make_async_copy(q_own, qx.at[me], q_sem)
    q_copy.start()

    @pl.loop(0, steps)
    def _(step):
        w_copy(step).start()

    barrier = pltpu.get_barrier_semaphore()
    peers = [(place(z_at(k), y, core), x) for k in range(1, depth)]
    peers += [(place(z, y_at(k), core), x) for k in range(1, ROWS)]
    peers += [(place(z, y, lax.rem(g_at(k), CORES)), lax.div(g_at(k), CORES)) for k in range(1, group)]
    for peer in peers:
        pl.semaphore_signal(barrier, inc=1, device_id=peer, device_id_type=MESH)

    rows = hidden.shape[0]
    hit = (iota((rows, tokens), 0) == target[...]).astype(F32).astype(BF16)
    onehot[...] = hit
    picked[...] = dot(hit, hidden[...], TN).astype(BF16)

    q_copy.wait()
    pl.semaphore_wait(barrier, len(peers))

    def remote(src, dst, send, recv, peer):
        return pltpu.make_async_remote_copy(
            src_ref=src, dst_ref=dst, send_sem=send, recv_sem=recv, device_id=peer, device_id_type=MESH
        )

    def z_copy(k):
        return remote(
            qx.at[me],
            qx.at[me],
            z_send.at[k],
            z_recv.at[k],
            (place(z_at(distance(k)), y, core), x),
        )

    def from_z(k):
        return z_at(depth - distance(k))

    def z_arrival(k):
        spot = qx.at[place(from_z(k), y, core)]
        return remote(spot, spot, z_send.at[k], z_recv.at[k], (place(from_z(k), y, core), x))

    def y_copy(k, j):
        spot = qx.at[place(from_z(k), y, core)]
        return remote(spot, spot, y_send.at[k, j], y_recv.at[k, j], (place(z, y_at(j), core), x))

    def y_arrival(k, j):
        spot = qx.at[place(from_z(k), y_at(ROWS - j), core)]
        return remote(
            spot, spot, y_send.at[k, j], y_recv.at[k, j], (place(z, y_at(ROWS - j), core), x)
        )

    def c_copy(k, j):
        spot = qx.at[place(from_z(k), y_at(ROWS - j), core)]
        return remote(spot, spot, c_send.at[k, j], c_recv.at[k, j], (place(z, y, other), x))

    def c_arrival(k, j):
        spot = qx.at[place(from_z(k), y_at(ROWS - j), other)]
        return remote(spot, spot, c_send.at[k, j], c_recv.at[k, j], (place(z, y, other), x))

    def spread(k):
        for j in range(1, ROWS):
            y_copy(k, j).start()
        c_copy(k, 0).start()

    def handed(k):
        for j in range(1, ROWS):
            y_arrival(k, j).wait_recv()
            c_copy(k, j).start()

    @pl.loop(1, depth)
    def _(k):
        z_copy(k).start()

    spread(0)

    @pl.loop(0, steps)
    def _(step):
        w_copy(step).wait()
        span = pl.ds(pl.multiple_of(step * FORWARD, FORWARD), FORWARD)
        grown = jnp.maximum(dot(picked[...], w[:, span], NN) + bias[:, span], 1.0)
        product = grown[:count]
        for t in range(1, picks):
            product = product * grown[t * count : (t + 1) * count]
        rep[:, span] = jnp.log(product).astype(BF16)
        inv[:, span] = jnp.where(grown > 1.0, 1.0 / grown, 0.0).astype(BF16)

        @pl.when(step < depth - 1)
        def _():
            k = step + 1
            z_arrival(k).wait_recv()
            spread(k)
            handed(k - 1)

    wide = QUARTERS * count
    slot = me * count + lax.rem(iota((wide, docs_total), 0), count)
    lane = iota((wide, docs_total), 1)
    order = jnp.zeros((wide, docs_total), jnp.int32)
    for r in range(slots.shape[0]):
        order = order + jnp.where(slots[r : r + 1, :] == slot, lane + r * docs_total, 0)
    order = jnp.sum(order.astype(F32), axis=1, keepdims=True)
    upto = (iota((docs_total, docs_total), 0) <= iota((docs_total, docs_total), 1)).astype(F32).astype(BF16)
    amount = jnp.broadcast_to(counts[...].astype(F32), (8, docs_total))
    ends = dot(amount.astype(BF16), upto, NN)[:1]
    begins = ends - amount[:1]
    member = ((order >= begins) & (order < ends)).astype(F32).astype(BF16)
    diagonal = iota((wide, wide), 0) == iota((wide, wide), 1)
    weight_row = weights[...]
    weight_column = jnp.sum(jnp.where(diagonal, weight_row, 0.0), axis=1, keepdims=True)
    stacked = qx.shape[0] * qx.shape[1]
    per = qx.shape[1]
    each = per // QUARTERS
    one, two = iota((docs_total, stacked), 0), iota((docs_total, stacked), 1)
    select = (lax.div(one, each) == lax.div(two, per)) & (lax.rem(one, each) == lax.rem(two, each))
    select = select.astype(F32).astype(BF16)

    handed(depth - 1)

    @pl.loop(0, depth)
    def _(k):
        for j in range(ROWS):
            c_arrival(k, j).wait_recv()

    queries = qx[...].reshape(stacked, quarter)
    reps = jnp.concatenate([rep[:, i * quarter : (i + 1) * quarter] for i in range(QUARTERS)], axis=0)
    pair = dot(queries, reps, NT)
    row, column = iota((stacked, wide), 0), iota((stacked, wide), 1)
    pair = jnp.where(
        lax.rem(lax.div(row, each), QUARTERS) == lax.div(column, count), pair * weight_row, 0.0
    )
    high, low = halves(pair)
    paired = dot(select, high, NN) + dot(select, low, NN)
    high, low = halves(paired)
    parts[...] = dot(high, member, NN) + dot(low, member, NN)

    def group_peer(k):
        return (place(z, y, lax.rem(k, CORES)), lax.div(k, CORES))

    def rows_of(k):
        return pl.ds(pl.multiple_of(k * share, share), share)

    def a_copy(k):
        to = g_at(k)
        return remote(parts.at[rows_of(to)], box_a.at[g], a_send.at[k], a_recv.at[g], group_peer(to))

    def a_arrival(k):
        frm = g_at(k)
        return remote(box_a.at[frm], box_a.at[frm], a_send.at[k], a_recv.at[frm], group_peer(frm))

    for k in range(1, group):
        a_copy(k).start()
    box_a[g] = parts[rows_of(g), :]
    for k in range(1, group):
        a_arrival(k).wait_recv()
    box_b[y] = jnp.sum(box_a[...], axis=0)

    def b_copy(k):
        return remote(
            box_b.at[y], box_b.at[y], b_send.at[k], b_recv.at[y], (place(z, y_at(k), core), x)
        )

    def b_arrival(k):
        frm = y_at(k)
        return remote(
            box_b.at[frm], box_b.at[frm], b_send.at[k], b_recv.at[frm], (place(z, frm, core), x)
        )

    for k in range(1, ROWS):
        b_copy(k).start()
    for k in range(1, ROWS):
        b_arrival(k).wait_recv()
    box_c[z] = jnp.sum(box_b[...], axis=0)

    def d_copy(k):
        return remote(
            box_c.at[z], box_c.at[z], d_send.at[k], d_recv.at[z], (place(z_at(k), y, core), x)
        )

    def d_arrival(k):
        frm = z_at(k)
        return remote(
            box_c.at[frm], box_c.at[frm], d_send.at[k], d_recv.at[frm], (place(frm, y, core), x)
        )

    for k in range(1, depth):
        d_copy(k).start()
    for k in range(1, depth):
        d_arrival(k).wait_recv()
    scores[rows_of(g), :] = jnp.sum(box_c[...], axis=0)

    def e_copy(k):
        mine = scores.at[rows_of(g)]
        return remote(mine, mine, e_send.at[k], e_recv.at[g], group_peer(g_at(k)))

    def e_arrival(k):
        frm = g_at(k)
        theirs = scores.at[rows_of(frm)]
        return remote(theirs, theirs, e_send.at[k], e_recv.at[frm], group_peer(frm))

    for k in range(1, group):
        e_copy(k).start()
    for k in range(1, group):
        e_arrival(k).wait_recv()

    score = scores[...]
    shape = (docs_total, docs_total)
    owned = scores_out.shape[0]
    for r in range(owned):
        scores_out[r : r + 1, :] = jnp.sum(
            jnp.where(iota(shape, 0) == me * owned + r, score, 0.0), axis=0, keepdims=True
        )
    power = jnp.exp(score - jnp.max(score, axis=1, keepdims=True))
    prob = power / jnp.sum(power, axis=1, keepdims=True)
    dscore = (prob - (iota(shape, 0) == iota(shape, 1)).astype(F32)) / docs_total

    high, low = halves(dscore)
    per_query = (dot(member, high, NT) + dot(member, low, NT)) * weight_column
    high, low = halves(per_query)
    spread_out = dot(jnp.concatenate([high, low], axis=0), select, NN)
    row, column = iota((2 * wide, stacked), 0), iota((2 * wide, stacked), 1)
    keep = lax.rem(lax.div(row, count), QUARTERS) == lax.rem(lax.div(column, each), QUARTERS)
    spread_out = jnp.where(keep, spread_out, 0.0).astype(BF16)
    cut = 5 * 128

    @pl.loop(0, quarter // cut)
    def _(i):
        span = pl.ds(pl.multiple_of(i * cut, cut), cut)
        found = dot(spread_out, qx[:, :, span].reshape(stacked, cut), NN)
        found = found[:wide] + found[wide:]
        for part in range(QUARTERS):
            there = pl.ds(pl.multiple_of(part * quarter + i * cut, 128), cut)
            value = found[part * count : (part + 1) * count]
            for t in range(picks):
                lines = slice(t * count, (t + 1) * count)
                inv[lines, there] = (inv[lines, there].astype(F32) * value).astype(BF16)

    def block_rows(k):
        return pl.ds(pl.multiple_of(k * piece_rows, piece_rows), piece_rows)

    def x_peer(k):
        return (me, k)

    def r_copy(j, k):
        to = x_at(k)
        return remote(
            part_send.at[j, block_rows(to)],
            part_box.at[j, x],
            r_send.at[j, k],
            r_recv.at[j, x],
            x_peer(to),
        )

    def r_arrival(j, k):
        frm = x_at(k)
        spot = part_box.at[j, frm]
        return remote(spot, spot, r_send.at[j, k], r_recv.at[j, frm], x_peer(frm))

    def t_copy(j, k):
        mine = total.at[j, block_rows(x)]
        return remote(mine, mine, g_send.at[j, k], g_recv.at[j, x], x_peer(x_at(k)))

    def t_arrival(j, k):
        frm = x_at(k)
        theirs = total.at[j, block_rows(frm)]
        return remote(theirs, theirs, g_send.at[j, k], g_recv.at[j, frm], x_peer(frm))

    def finish(j):
        value = part_own[j, block_rows(x), :]
        for k in range(1, blocks):
            r_arrival(j, k).wait_recv()
            value = value + part_box[j, x_at(k)].astype(F32)
        total[j, block_rows(x), :] = value.astype(BF16)
        for k in range(1, blocks):
            t_copy(j, k).start()

    @pl.loop(0, 3)
    def _(j):
        span = pl.ds(pl.multiple_of(j * columns, columns), columns)
        value = dot(inv[...], w[span, :], NT)
        part_own[j] = value
        part_send[j] = value.astype(BF16)
        for k in range(1, blocks):
            r_copy(j, k).start()

        @pl.when(j >= 1)
        def _():
            finish(j - 1)

    finish(2)

    for j in range(3):
        for k in range(1, blocks):
            t_arrival(j, k).wait_recv()
        grad_out[:, j * columns : (j + 1) * columns] = dot(onehot[...], total[j], NN).astype(BF16)

    @pl.loop(1, depth)
    def _(k):
        z_copy(k).wait_send()

    @pl.loop(0, depth)
    def _(k):
        for j in range(ROWS):
            if j:
                y_copy(k, j).wait_send()
            c_copy(k, j).wait_send()

    for k in range(1, group):
        a_copy(k).wait_send()
        e_copy(k).wait_send()
    for k in range(1, ROWS):
        b_copy(k).wait_send()
    for k in range(1, depth):
        d_copy(k).wait_send()
    for j in range(3):
        for k in range(1, blocks):
            r_copy(j, k).wait_send()
            t_copy(j, k).wait_send()


def solution(mesh):
    passes, blocks = mesh.shape["pass"], mesh.shape["voc"]
    depth = passes // (ROWS * CORES)
    group = blocks * CORES

    def on_device(
        hidden, positions, passage_weight, passage_counts, passage_slot, head_weight, head_bias, queries
    ):
        count, length, width = hidden.shape
        picks = positions.shape[1]
        tokens = count * picks
        docs = passage_counts.shape[0]
        vocab = head_weight.shape[1]
        owned = queries.shape[0]
        quarter = vocab // QUARTERS
        per = QUARTERS * owned
        share = docs // group
        columns = width // 3
        target = (positions + length * jnp.arange(count, dtype=jnp.int32)[:, None]).T.reshape(1, tokens)
        piece = queries.reshape(owned, QUARTERS, quarter).transpose(1, 0, 2).reshape(per, quarter)
        vmem = pl.BlockSpec(memory_space=pltpu.VMEM)
        dma = pltpu.SemaphoreType.DMA
        scores, grad = pl.pallas_call(
            functools.partial(kernel, depth, blocks),
            out_shape=(
                jax.ShapeDtypeStruct((owned, docs), F32),
                jax.ShapeDtypeStruct((count * length, width), BF16),
            ),
            in_specs=[vmem, vmem, vmem, vmem, vmem, pl.BlockSpec(memory_space=pl.ANY), vmem, vmem],
            out_specs=(vmem, vmem),
            scratch_shapes=[
                pltpu.VMEM((width, vocab), BF16),
                pltpu.VMEM((tokens, vocab), BF16),
                pltpu.VMEM((count, vocab), BF16),
                pltpu.VMEM((8, 128), F32),
                pltpu.VMEM((passes, per, quarter), BF16),
                pltpu.VMEM((tokens, width), BF16),
                pltpu.VMEM((count * length, tokens), BF16),
                pltpu.VMEM((docs, docs), F32),
                pltpu.VMEM((group, share, docs), F32),
                pltpu.VMEM((ROWS, share, docs), F32),
                pltpu.VMEM((depth, share, docs), F32),
                pltpu.VMEM((docs, docs), F32),
                pltpu.VMEM((3, tokens, columns), F32),
                pltpu.VMEM((3, tokens, columns), BF16),
                pltpu.VMEM((3, blocks, tokens // blocks, columns), BF16),
                pltpu.VMEM((3, tokens, columns), BF16),
                dma((vocab // FORWARD,)),
                dma,
                dma((depth,)),
                dma((depth,)),
                dma((depth, ROWS)),
                dma((depth, ROWS)),
                dma((depth, ROWS)),
                dma((depth, ROWS)),
                dma((group,)),
                dma((group,)),
                dma((ROWS,)),
                dma((ROWS,)),
                dma((depth,)),
                dma((depth,)),
                dma((group,)),
                dma((group,)),
                dma((3, blocks)),
                dma((3, blocks)),
                dma((3, blocks)),
                dma((3, blocks)),
            ],
            compiler_params=pltpu.CompilerParams(collective_id=0, has_side_effects=True),
        )(
            hidden.reshape(count * length, width),
            target,
            jnp.tile(passage_weight, QUARTERS).reshape(1, QUARTERS * count),
            passage_counts.reshape(1, docs),
            passage_slot.reshape(-1, docs),
            head_weight,
            (head_bias + 1.0).reshape(1, vocab),
            piece,
        )
        return scores, grad.reshape(count, length, width)

    placed = (
        P("pass", None, None),
        P("pass", None),
        P("pass"),
        P(),
        P(),
        P(None, "voc"),
        P("voc"),
        P("pass", "voc"),
    )
    return jax.shard_map(
        on_device,
        mesh=mesh,
        in_specs=placed,
        out_specs=(P("pass", None), P("pass", None, None)),
        check_vma=False,
    )
```

```python
import functools

import jax
import jax.numpy as jnp
from jax import lax
from jax.experimental import pallas as pl
from jax.experimental.pallas import tpu as pltpu
from jax.sharding import PartitionSpec as P

MESH = pl.DeviceIdType.MESH
CORES = 2
ROWS = 4
QUARTERS = 4
FORWARD = 512
LAG = 3
AWAY = (1, 3)
HALF = (pl.ds(0, 1024), pl.ds(1024, 896))
F32 = jnp.float32
BF16 = jnp.bfloat16
NT = (((1,), (1,)), ((), ()))
NN = (((1,), (0,)), ((), ()))
TN = (((0,), (0,)), ((), ()))


def dot(a, b, dims):
    return lax.dot_general(a, b, dims, preferred_element_type=F32)


def halves(a):
    high = a.astype(BF16)
    return high, (a - high.astype(F32)).astype(BF16)


def iota(shape, dim):
    return lax.broadcasted_iota(jnp.int32, shape, dim)


def token_hits(positions, rows):
    picks, count = positions.shape
    tokens = picks * count
    passage = (iota((count, tokens), 0) == lax.rem(iota((count, tokens), 1), count)).astype(F32)
    spread = dot(positions[...].astype(F32).astype(BF16), passage.astype(BF16), NN)
    own = iota((picks, tokens), 0) == lax.div(iota((picks, tokens), 1), count)
    chosen = jnp.sum(jnp.where(own, spread, 0.0), axis=0, keepdims=True).astype(jnp.int32)
    length = rows // count
    goal = chosen + length * lax.rem(iota((1, tokens), 1), count)
    return (iota((rows, tokens), 0) == goal).astype(F32).astype(BF16)


def expand(positions, sums, scores, grad_out, scores_out):
    scores_out[...] = scores[...]
    hits = token_hits(positions, grad_out.shape[0])
    columns = sums.shape[2]
    for j in range(sums.shape[0]):
        grad_out[:, j * columns : (j + 1) * columns] = dot(hits, sums[j], NN).astype(BF16)


def kernel(
    depth,
    blocks,
    hidden_hbm,
    positions_hbm,
    weights_hbm,
    counts_hbm,
    slots_hbm,
    w_hbm,
    bias_hbm,
    q_hbm,
    scores_out,
    total,
    w,
    inv,
    rep,
    piece,
    qx,
    picked,
    parts,
    box_a,
    box_b,
    box_c,
    scores,
    part_own,
    part_send,
    part_box,
    hidden,
    positions,
    weights,
    counts,
    slots,
    bias,
    q_own,
    in_sem,
    w_sem,
    q_sem,
    z_send,
    z_recv,
    y_send,
    y_recv,
    h_send,
    h_recv,
    c_send,
    c_recv,
    a_send,
    a_recv,
    b_send,
    b_recv,
    d_send,
    d_recv,
    e_send,
    e_recv,
    r_send,
    r_recv,
    g_send,
    g_recv,
):
    me = lax.axis_index("pass")
    x = lax.axis_index("voc")
    core = lax.rem(me, CORES)
    y = lax.rem(lax.div(me, CORES), ROWS)
    z = lax.div(me, CORES * ROWS)
    group = blocks * CORES
    g = x * CORES + core
    vocab = w.shape[1]
    width = w.shape[0]
    count = rep.shape[0]
    picks = picked.shape[0] // count
    docs_total = counts.shape[1]
    quarter = vocab // QUARTERS
    share = docs_total // group
    steps = vocab // FORWARD
    columns = width // 3
    tokens = picked.shape[0]
    piece_rows = tokens // blocks

    def place(zz, yy, cc):
        return (zz * ROWS + yy) * CORES + cc

    def z_at(k):
        return lax.rem(z + k, depth)

    def y_at(k):
        return lax.rem(y + k, ROWS)

    def x_at(k):
        return lax.rem(x + k, blocks)

    def g_at(k):
        return lax.rem(g + k, group)

    def distance(k):
        odd = lax.rem(k, 2)
        return odd * lax.div(k + 1, 2) + (1 - odd) * lax.rem(depth - lax.div(k, 2), depth)

    other = 1 - core

    barrier = pltpu.get_barrier_semaphore()
    peers = [(place(z_at(k), y, core), x) for k in range(1, depth)]
    peers += [(place(z, y_at(k), core), x) for k in range(1, ROWS)]
    peers += [(place(z, y, lax.rem(g_at(k), CORES)), lax.div(g_at(k), CORES)) for k in range(1, group)]
    for peer in peers:
        pl.semaphore_signal(barrier, inc=1, device_id=peer, device_id_type=MESH)

    small = [
        pltpu.make_async_copy(src, dst, in_sem.at[i])
        for i, (src, dst) in enumerate(
            (
                (q_hbm, q_own),
                (positions_hbm, positions),
                (hidden_hbm, hidden),
                (weights_hbm, weights),
                (counts_hbm, counts),
                (slots_hbm, slots),
                (bias_hbm, bias),
            )
        )
    ]
    for copy in small:
        copy.start()

    def w_copy(step):
        span = pl.ds(pl.multiple_of(step * FORWARD, FORWARD), FORWARD)
        return pltpu.make_async_copy(w_hbm.at[:, span], w.at[:, span], w_sem.at[step])

    @pl.loop(0, steps)
    def _(step):
        w_copy(step).start()

    small[0].wait()
    piece[...] = jnp.concatenate([q_own[i] for i in range(QUARTERS)], axis=0)
    q_copy = pltpu.make_async_copy(piece, qx.at[me], q_sem)
    q_copy.start()

    for copy in small[1:]:
        copy.wait()
    picked[...] = dot(token_hits(positions, hidden.shape[0]), hidden[...], TN).astype(BF16)

    q_copy.wait()
    pl.semaphore_wait(barrier, len(peers))

    def remote(src, dst, send, recv, peer):
        return pltpu.make_async_remote_copy(
            src_ref=src, dst_ref=dst, send_sem=send, recv_sem=recv, device_id=peer, device_id_type=MESH
        )

    def z_copy(k):
        return remote(
            qx.at[me],
            qx.at[me],
            z_send.at[k],
            z_recv.at[k],
            (place(z_at(distance(k)), y, core), x),
        )

    def from_z(k):
        return z_at(depth - distance(k))

    def z_arrival(k):
        spot = qx.at[place(from_z(k), y, core)]
        return remote(spot, spot, z_send.at[k], z_recv.at[k], (place(from_z(k), y, core), x))

    def y_copy(k, j):
        spot = qx.at[place(from_z(k), y, core)]
        return remote(spot, spot, y_send.at[k, j], y_recv.at[k, j], (place(z, y_at(AWAY[j]), core), x))

    def y_arrival(k, j):
        frm = y_at(ROWS - AWAY[j])
        spot = qx.at[place(from_z(k), frm, core)]
        return remote(spot, spot, y_send.at[k, j], y_recv.at[k, j], (place(z, frm, core), x))

    def h_copy(k, j):
        spot = qx.at[place(from_z(k), y_at(ROWS - AWAY[j]), core), :, HALF[j]]
        return remote(spot, spot, h_send.at[k, j], h_recv.at[k, j], (place(z, y_at(AWAY[j]), core), x))

    def h_arrival(k, j):
        spot = qx.at[place(from_z(k), y_at(2), core), :, HALF[j]]
        frm = y_at(ROWS - AWAY[j])
        return remote(spot, spot, h_send.at[k, j], h_recv.at[k, j], (place(z, frm, core), x))

    def c_copy(k, j):
        spot = qx.at[place(from_z(k), y_at(j), core)]
        return remote(spot, spot, c_send.at[k, j], c_recv.at[k, j], (place(z, y, other), x))

    def c_arrival(k, j):
        spot = qx.at[place(from_z(k), y_at(j), other)]
        return remote(spot, spot, c_send.at[k, j], c_recv.at[k, j], (place(z, y, other), x))

    def spread(k):
        for j in range(2):
            y_copy(k, j).start()
        c_copy(k, 0).start()

    def handed(k):
        for j in range(2):
            y_arrival(k, j).wait_recv()
            h_copy(k, j).start()
            c_copy(k, ROWS - AWAY[j]).start()

    def relayed(k):
        for j in range(2):
            h_arrival(k, j).wait_recv()
        c_copy(k, 2).start()

    @pl.loop(1, depth)
    def _(k):
        z_copy(k).start()

    spread(0)

    @pl.loop(0, steps)
    def _(step):
        w_copy(step).wait()
        span = pl.ds(pl.multiple_of(step * FORWARD, FORWARD), FORWARD)
        lines = FORWARD // 128
        offset = jnp.concatenate([bias[pl.ds(step * lines + i, 1), :] for i in range(lines)], axis=1) + 1.0
        grown = jnp.maximum(dot(picked[...], w[:, span], NN) + offset, 1.0)
        product = grown[:count]
        for t in range(1, picks):
            product = product * grown[t * count : (t + 1) * count]
        rep[:, span] = jnp.log(product).astype(BF16)
        inv[:, span] = jnp.where(grown > 1.0, 1.0 / grown, 0.0).astype(BF16)

        @pl.when(step < depth - 1)
        def _():
            z_arrival(step + 1).wait_recv()
            spread(step + 1)

        @pl.when((step >= LAG) & (step < depth + LAG))
        def _():
            handed(step - LAG)

        @pl.when((step >= 2 * LAG) & (step < depth + 2 * LAG))
        def _():
            relayed(step - 2 * LAG)

    wide = QUARTERS * count
    slot = me * count + lax.rem(iota((wide, docs_total), 0), count)
    lane = iota((wide, docs_total), 1)
    order = jnp.zeros((wide, docs_total), jnp.int32)
    for r in range(slots.shape[0]):
        order = order + jnp.where(slots[r : r + 1, :] == slot, lane + r * docs_total, 0)
    order = jnp.sum(order.astype(F32), axis=1, keepdims=True)
    upto = (iota((docs_total, docs_total), 0) <= iota((docs_total, docs_total), 1)).astype(F32).astype(BF16)
    amount = jnp.broadcast_to(counts[...].astype(F32), (8, docs_total))
    ends = dot(amount.astype(BF16), upto, NN)[:1]
    begins = ends - amount[:1]
    member = ((order >= begins) & (order < ends)).astype(F32).astype(BF16)
    diagonal = iota((count, count), 0) == iota((count, count), 1)
    weight_column = jnp.sum(jnp.where(diagonal, weights[...], 0.0), axis=1, keepdims=True)
    weight_column = jnp.concatenate([weight_column] * QUARTERS, axis=0)
    diagonal = iota((wide, wide), 0) == iota((wide, wide), 1)
    weight_row = jnp.sum(jnp.where(diagonal, weight_column, 0.0), axis=0, keepdims=True)
    stacked = qx.shape[0] * qx.shape[1]
    per = qx.shape[1]
    each = per // QUARTERS
    one, two = iota((docs_total, stacked), 0), iota((docs_total, stacked), 1)
    select = (lax.div(one, each) == lax.div(two, per)) & (lax.rem(one, each) == lax.rem(two, each))
    select = select.astype(F32).astype(BF16)

    for k in range(steps - 2 * LAG, depth):
        relayed(k)

    @pl.loop(0, depth)
    def _(k):
        for j in range(ROWS):
            c_arrival(k, j).wait_recv()

    queries = qx[...].reshape(stacked, quarter)
    reps = jnp.concatenate([rep[:, i * quarter : (i + 1) * quarter] for i in range(QUARTERS)], axis=0)
    pair = dot(queries, reps, NT)
    row, column = iota((stacked, wide), 0), iota((stacked, wide), 1)
    pair = jnp.where(
        lax.rem(lax.div(row, each), QUARTERS) == lax.div(column, count), pair * weight_row, 0.0
    )
    high, low = halves(pair)
    paired = dot(select, high, NN) + dot(select, low, NN)
    high, low = halves(paired)
    parts[...] = dot(high, member, NN) + dot(low, member, NN)

    def group_peer(k):
        return (place(z, y, lax.rem(k, CORES)), lax.div(k, CORES))

    def rows_of(k):
        return pl.ds(pl.multiple_of(k * share, share), share)

    def a_copy(k):
        to = g_at(k)
        return remote(parts.at[rows_of(to)], box_a.at[g], a_send.at[k], a_recv.at[g], group_peer(to))

    def a_arrival(k):
        frm = g_at(k)
        return remote(box_a.at[frm], box_a.at[frm], a_send.at[k], a_recv.at[frm], group_peer(frm))

    for k in range(1, group):
        a_copy(k).start()
    box_a[g] = parts[rows_of(g), :]
    for k in range(1, group):
        a_arrival(k).wait_recv()
    box_b[y] = jnp.sum(box_a[...], axis=0)

    def b_copy(k):
        return remote(
            box_b.at[y], box_b.at[y], b_send.at[k], b_recv.at[y], (place(z, y_at(k), core), x)
        )

    def b_arrival(k):
        frm = y_at(k)
        return remote(
            box_b.at[frm], box_b.at[frm], b_send.at[k], b_recv.at[frm], (place(z, frm, core), x)
        )

    for k in range(1, ROWS):
        b_copy(k).start()
    for k in range(1, ROWS):
        b_arrival(k).wait_recv()
    box_c[z] = jnp.sum(box_b[...], axis=0)

    def d_copy(k):
        return remote(
            box_c.at[z], box_c.at[z], d_send.at[k], d_recv.at[z], (place(z_at(k), y, core), x)
        )

    def d_arrival(k):
        frm = z_at(k)
        return remote(
            box_c.at[frm], box_c.at[frm], d_send.at[k], d_recv.at[frm], (place(frm, y, core), x)
        )

    for k in range(1, depth):
        d_copy(k).start()
    for k in range(1, depth):
        d_arrival(k).wait_recv()
    scores[rows_of(g), :] = jnp.sum(box_c[...], axis=0)

    def e_copy(k):
        mine = scores.at[rows_of(g)]
        return remote(mine, mine, e_send.at[k], e_recv.at[g], group_peer(g_at(k)))

    def e_arrival(k):
        frm = g_at(k)
        theirs = scores.at[rows_of(frm)]
        return remote(theirs, theirs, e_send.at[k], e_recv.at[frm], group_peer(frm))

    for k in range(1, group):
        e_copy(k).start()
    for k in range(1, group):
        e_arrival(k).wait_recv()

    score = scores[...]
    shape = (docs_total, docs_total)
    owned = scores_out.shape[0]
    for r in range(owned):
        scores_out[r : r + 1, :] = jnp.sum(
            jnp.where(iota(shape, 0) == me * owned + r, score, 0.0), axis=0, keepdims=True
        )
    power = jnp.exp(score - jnp.max(score, axis=1, keepdims=True))
    prob = power / jnp.sum(power, axis=1, keepdims=True)
    dscore = (prob - (iota(shape, 0) == iota(shape, 1)).astype(F32)) / docs_total

    high, low = halves(dscore)
    per_query = (dot(member, high, NT) + dot(member, low, NT)) * weight_column
    high, low = halves(per_query)
    spread_out = dot(jnp.concatenate([high, low], axis=0), select, NN)
    row, column = iota((2 * wide, stacked), 0), iota((2 * wide, stacked), 1)
    keep = lax.rem(lax.div(row, count), QUARTERS) == lax.rem(lax.div(column, each), QUARTERS)
    spread_out = jnp.where(keep, spread_out, 0.0).astype(BF16)
    cut = 5 * 128

    @pl.loop(0, quarter // cut)
    def _(i):
        span = pl.ds(pl.multiple_of(i * cut, cut), cut)
        found = dot(spread_out, qx[:, :, span].reshape(stacked, cut), NN)
        found = found[:wide] + found[wide:]
        for part in range(QUARTERS):
            there = pl.ds(pl.multiple_of(part * quarter + i * cut, 128), cut)
            value = found[part * count : (part + 1) * count]
            for t in range(picks):
                lines = slice(t * count, (t + 1) * count)
                inv[lines, there] = (inv[lines, there].astype(F32) * value).astype(BF16)

    def block_rows(k):
        return pl.ds(pl.multiple_of(k * piece_rows, piece_rows), piece_rows)

    def x_peer(k):
        return (me, k)

    def r_copy(j, k):
        to = x_at(k)
        return remote(
            part_send.at[j, block_rows(to)],
            part_box.at[j, x],
            r_send.at[j, k],
            r_recv.at[j, x],
            x_peer(to),
        )

    def r_arrival(j, k):
        frm = x_at(k)
        spot = part_box.at[j, frm]
        return remote(spot, spot, r_send.at[j, k], r_recv.at[j, frm], x_peer(frm))

    def t_copy(j, k):
        mine = total.at[j, block_rows(x)]
        return remote(mine, mine, g_send.at[j, k], g_recv.at[j, x], x_peer(x_at(k)))

    def t_arrival(j, k):
        frm = x_at(k)
        theirs = total.at[j, block_rows(frm)]
        return remote(theirs, theirs, g_send.at[j, k], g_recv.at[j, frm], x_peer(frm))

    def finish(j):
        value = part_own[j, block_rows(x), :]
        for k in range(1, blocks):
            r_arrival(j, k).wait_recv()
            value = value + part_box[j, x_at(k)].astype(F32)
        total[j, block_rows(x), :] = value.astype(BF16)
        for k in range(1, blocks):
            t_copy(j, k).start()

    @pl.loop(0, 3)
    def _(j):
        span = pl.ds(pl.multiple_of(j * columns, columns), columns)
        value = dot(inv[...], w[span, :], NT)
        part_own[j] = value
        part_send[j] = value.astype(BF16)
        for k in range(1, blocks):
            r_copy(j, k).start()

        @pl.when(j >= 1)
        def _():
            finish(j - 1)

    finish(2)

    for j in range(3):
        for k in range(1, blocks):
            t_arrival(j, k).wait_recv()

    @pl.loop(1, depth)
    def _(k):
        z_copy(k).wait_send()

    @pl.loop(0, depth)
    def _(k):
        for j in range(2):
            y_copy(k, j).wait_send()
            h_copy(k, j).wait_send()
        for j in range(ROWS):
            c_copy(k, j).wait_send()

    for k in range(1, group):
        a_copy(k).wait_send()
        e_copy(k).wait_send()
    for k in range(1, ROWS):
        b_copy(k).wait_send()
    for k in range(1, depth):
        d_copy(k).wait_send()
    for j in range(3):
        for k in range(1, blocks):
            r_copy(j, k).wait_send()
            t_copy(j, k).wait_send()


def solution(mesh):
    passes, blocks = mesh.shape["pass"], mesh.shape["voc"]
    depth = passes // (ROWS * CORES)
    group = blocks * CORES

    def on_device(
        hidden, positions, passage_weight, passage_counts, passage_slot, head_weight, head_bias, queries
    ):
        count, length, width = hidden.shape
        picks = positions.shape[1]
        tokens = count * picks
        docs = passage_counts.shape[0]
        vocab = head_weight.shape[1]
        owned = queries.shape[0]
        quarter = vocab // QUARTERS
        per = QUARTERS * owned
        share = docs // group
        columns = width // 3
        piece = queries.reshape(owned, QUARTERS, quarter).transpose(1, 0, 2)
        vmem = pl.BlockSpec(memory_space=pltpu.VMEM)
        anywhere = pl.BlockSpec(memory_space=pl.ANY)
        dma = pltpu.SemaphoreType.DMA
        scores, sums = pl.pallas_call(
            functools.partial(kernel, depth, blocks),
            out_shape=(
                jax.ShapeDtypeStruct((owned, docs), F32),
                jax.ShapeDtypeStruct((3, tokens, columns), BF16),
            ),
            in_specs=[anywhere] * 8,
            out_specs=(vmem, vmem),
            scratch_shapes=[
                pltpu.VMEM((width, vocab), BF16),
                pltpu.VMEM((tokens, vocab), BF16),
                pltpu.VMEM((count, vocab), BF16),
                pltpu.VMEM((per, quarter), BF16),
                pltpu.VMEM((passes, per, quarter), BF16),
                pltpu.VMEM((tokens, width), BF16),
                pltpu.VMEM((docs, docs), F32),
                pltpu.VMEM((group, share, docs), F32),
                pltpu.VMEM((ROWS, share, docs), F32),
                pltpu.VMEM((depth, share, docs), F32),
                pltpu.VMEM((docs, docs), F32),
                pltpu.VMEM((3, tokens, columns), F32),
                pltpu.VMEM((3, tokens, columns), BF16),
                pltpu.VMEM((3, blocks, tokens // blocks, columns), BF16),
                pltpu.VMEM((count * length, width), BF16),
                pltpu.VMEM((picks, count), jnp.int32),
                pltpu.VMEM((1, count), F32),
                pltpu.VMEM((1, docs), jnp.int32),
                pltpu.VMEM((passage_slot.shape[0] // docs, docs), jnp.int32),
                pltpu.VMEM((vocab // 128, 128), F32),
                pltpu.VMEM((QUARTERS, owned, quarter), BF16),
                dma((7,)),
                dma((vocab // FORWARD,)),
                dma,
                dma((depth,)),
                dma((depth,)),
                dma((depth, 2)),
                dma((depth, 2)),
                dma((depth, 2)),
                dma((depth, 2)),
                dma((depth, ROWS)),
                dma((depth, ROWS)),
                dma((group,)),
                dma((group,)),
                dma((ROWS,)),
                dma((ROWS,)),
                dma((depth,)),
                dma((depth,)),
                dma((group,)),
                dma((group,)),
                dma((3, blocks)),
                dma((3, blocks)),
                dma((3, blocks)),
                dma((3, blocks)),
            ],
            compiler_params=pltpu.CompilerParams(collective_id=0, has_side_effects=True),
        )(
            hidden.reshape(count * length, width),
            positions.T,
            passage_weight.reshape(1, count),
            passage_counts.reshape(1, docs),
            passage_slot.reshape(-1, docs),
            head_weight,
            head_bias.reshape(vocab // 128, 128),
            piece,
        )
        grad, scores = pl.pallas_call(
            expand,
            out_shape=(
                jax.ShapeDtypeStruct((count * length, width), BF16),
                jax.ShapeDtypeStruct((owned, docs), F32),
            ),
            in_specs=[vmem] * 3,
            out_specs=(vmem, vmem),
        )(positions.T, sums, scores)
        return scores, grad.reshape(count, length, width)

    placed = (
        P("pass", None, None),
        P("pass", None),
        P("pass"),
        P(),
        P(),
        P(None, "voc"),
        P("voc"),
        P("pass", "voc"),
    )
    return jax.shard_map(
        on_device,
        mesh=mesh,
        in_specs=placed,
        out_specs=(P("pass", None), P("pass", None, None)),
        check_vma=False,
    )
```

```python
import functools

import jax
import jax.numpy as jnp
from jax import lax
from jax.experimental import pallas as pl
from jax.experimental.pallas import tpu as pltpu
from jax.sharding import PartitionSpec as P

MESH = pl.DeviceIdType.MESH
CORES = 2
ROWS = 4
QUARTERS = 4
FORWARD = 512
LAG = 3
AWAY = (1, 3)
HALF = (pl.ds(0, 1024), pl.ds(1024, 896))
F32 = jnp.float32
BF16 = jnp.bfloat16
NT = (((1,), (1,)), ((), ()))
NN = (((1,), (0,)), ((), ()))
TN = (((0,), (0,)), ((), ()))


def dot(a, b, dims):
    return lax.dot_general(a, b, dims, preferred_element_type=F32)


def halves(a):
    high = a.astype(BF16)
    return high, (a - high.astype(F32)).astype(BF16)


def iota(shape, dim):
    return lax.broadcasted_iota(jnp.int32, shape, dim)


def token_hits(positions, rows):
    picks, count = positions.shape
    tokens = picks * count
    passage = (iota((count, tokens), 0) == lax.rem(iota((count, tokens), 1), count)).astype(F32)
    spread = dot(positions[...].astype(F32).astype(BF16), passage.astype(BF16), NN)
    own = iota((picks, tokens), 0) == lax.div(iota((picks, tokens), 1), count)
    chosen = jnp.sum(jnp.where(own, spread, 0.0), axis=0, keepdims=True).astype(jnp.int32)
    length = rows // count
    goal = chosen + length * lax.rem(iota((1, tokens), 1), count)
    return (iota((rows, tokens), 0) == goal).astype(F32).astype(BF16)


def expand(hits, sums, scores, grad_hbm, scores_out, grad, out_sem):
    scores_out[...] = scores[...]
    pieces, rows, _ = grad.shape
    columns = sums.shape[2]
    stores = []
    for i in range(pieces):
        lines = slice(i * rows, (i + 1) * rows)
        for j in range(sums.shape[0]):
            grad[i, :, j * columns : (j + 1) * columns] = dot(hits[lines, :], sums[j], NN).astype(BF16)
        store = pltpu.make_async_copy(grad.at[i], grad_hbm.at[pl.ds(i * rows, rows)], out_sem.at[i])
        store.start()
        stores.append(store)
    for store in stores:
        store.wait()


def kernel(
    depth,
    blocks,
    hidden_hbm,
    positions_hbm,
    weights_hbm,
    counts_hbm,
    slots_hbm,
    w_hbm,
    bias_hbm,
    q_hbm,
    scores_out,
    total,
    hits,
    w,
    inv,
    rep,
    piece,
    qx,
    picked,
    parts,
    box_a,
    box_b,
    box_c,
    scores,
    part_own,
    part_send,
    part_box,
    hidden,
    positions,
    weights,
    counts,
    slots,
    bias,
    q_own,
    in_sem,
    w_sem,
    q_sem,
    z_send,
    z_recv,
    y_send,
    y_recv,
    h_send,
    h_recv,
    c_send,
    c_recv,
    a_send,
    a_recv,
    b_send,
    b_recv,
    d_send,
    d_recv,
    e_send,
    e_recv,
    r_send,
    r_recv,
    g_send,
    g_recv,
):
    me = lax.axis_index("pass")
    x = lax.axis_index("voc")
    core = lax.rem(me, CORES)
    y = lax.rem(lax.div(me, CORES), ROWS)
    z = lax.div(me, CORES * ROWS)
    group = blocks * CORES
    g = x * CORES + core
    vocab = w.shape[1]
    width = w.shape[0]
    count = rep.shape[0]
    picks = picked.shape[0] // count
    docs_total = counts.shape[1]
    quarter = vocab // QUARTERS
    share = docs_total // group
    steps = vocab // FORWARD
    columns = width // 3
    tokens = picked.shape[0]
    lots = part_own.shape[0]
    piece_rows = tokens // blocks

    def place(zz, yy, cc):
        return (zz * ROWS + yy) * CORES + cc

    def z_at(k):
        return lax.rem(z + k, depth)

    def y_at(k):
        return lax.rem(y + k, ROWS)

    def x_at(k):
        return lax.rem(x + k, blocks)

    def g_at(k):
        return lax.rem(g + k, group)

    def distance(k):
        odd = lax.rem(k, 2)
        return odd * lax.div(k + 1, 2) + (1 - odd) * lax.rem(depth - lax.div(k, 2), depth)

    other = 1 - core

    barrier = pltpu.get_barrier_semaphore()
    peers = [(place(z_at(k), y, core), x) for k in range(1, depth)]
    peers += [(place(z, y_at(k), core), x) for k in range(1, ROWS)]
    peers += [(place(z, y, lax.rem(g_at(k), CORES)), lax.div(g_at(k), CORES)) for k in range(1, group)]
    for peer in peers:
        pl.semaphore_signal(barrier, inc=1, device_id=peer, device_id_type=MESH)

    small = [
        pltpu.make_async_copy(src, dst, in_sem.at[i])
        for i, (src, dst) in enumerate(
            (
                (q_hbm, q_own),
                (positions_hbm, positions),
                (hidden_hbm, hidden),
                (weights_hbm, weights),
                (counts_hbm, counts),
                (slots_hbm, slots),
                (bias_hbm, bias),
            )
        )
    ]
    for copy in small:
        copy.start()

    def w_copy(step):
        span = pl.ds(pl.multiple_of(step * FORWARD, FORWARD), FORWARD)
        return pltpu.make_async_copy(w_hbm.at[:, span], w.at[:, span], w_sem.at[step])

    @pl.loop(0, steps)
    def _(step):
        w_copy(step).start()

    small[0].wait()
    piece[...] = jnp.concatenate([q_own[i] for i in range(QUARTERS)], axis=0)
    q_copy = pltpu.make_async_copy(piece, qx.at[me], q_sem)
    q_copy.start()

    for copy in small[1:]:
        copy.wait()
    hit = token_hits(positions, hidden.shape[0])
    hits[...] = hit
    picked[...] = dot(hit, hidden[...], TN).astype(BF16)

    q_copy.wait()
    pl.semaphore_wait(barrier, len(peers))

    def remote(src, dst, send, recv, peer):
        return pltpu.make_async_remote_copy(
            src_ref=src, dst_ref=dst, send_sem=send, recv_sem=recv, device_id=peer, device_id_type=MESH
        )

    def z_copy(k):
        return remote(
            qx.at[me],
            qx.at[me],
            z_send.at[k],
            z_recv.at[k],
            (place(z_at(distance(k)), y, core), x),
        )

    def from_z(k):
        return z_at(depth - distance(k))

    def z_arrival(k):
        spot = qx.at[place(from_z(k), y, core)]
        return remote(spot, spot, z_send.at[k], z_recv.at[k], (place(from_z(k), y, core), x))

    def y_copy(k, j):
        spot = qx.at[place(from_z(k), y, core)]
        return remote(spot, spot, y_send.at[k, j], y_recv.at[k, j], (place(z, y_at(AWAY[j]), core), x))

    def y_arrival(k, j):
        frm = y_at(ROWS - AWAY[j])
        spot = qx.at[place(from_z(k), frm, core)]
        return remote(spot, spot, y_send.at[k, j], y_recv.at[k, j], (place(z, frm, core), x))

    def h_copy(k, j):
        spot = qx.at[place(from_z(k), y_at(ROWS - AWAY[j]), core), :, HALF[j]]
        return remote(spot, spot, h_send.at[k, j], h_recv.at[k, j], (place(z, y_at(AWAY[j]), core), x))

    def h_arrival(k, j):
        spot = qx.at[place(from_z(k), y_at(2), core), :, HALF[j]]
        frm = y_at(ROWS - AWAY[j])
        return remote(spot, spot, h_send.at[k, j], h_recv.at[k, j], (place(z, frm, core), x))

    def c_copy(k, j):
        spot = qx.at[place(from_z(k), y_at(j), core)]
        return remote(spot, spot, c_send.at[k, j], c_recv.at[k, j], (place(z, y, other), x))

    def c_arrival(k, j):
        spot = qx.at[place(from_z(k), y_at(j), other)]
        return remote(spot, spot, c_send.at[k, j], c_recv.at[k, j], (place(z, y, other), x))

    def spread(k):
        for j in range(2):
            y_copy(k, j).start()
        c_copy(k, 0).start()

    def handed(k):
        for j in range(2):
            y_arrival(k, j).wait_recv()
            h_copy(k, j).start()
            c_copy(k, ROWS - AWAY[j]).start()

    def relayed(k):
        for j in range(2):
            h_arrival(k, j).wait_recv()
        c_copy(k, 2).start()

    @pl.loop(1, depth)
    def _(k):
        z_copy(k).start()

    spread(0)

    @pl.loop(0, steps)
    def _(step):
        w_copy(step).wait()
        span = pl.ds(pl.multiple_of(step * FORWARD, FORWARD), FORWARD)
        lines = FORWARD // 128
        offset = jnp.concatenate([bias[pl.ds(step * lines + i, 1), :] for i in range(lines)], axis=1) + 1.0
        grown = jnp.maximum(dot(picked[...], w[:, span], NN) + offset, 1.0)
        product = grown[:count]
        for t in range(1, picks):
            product = product * grown[t * count : (t + 1) * count]
        rep[:, span] = jnp.log(product).astype(BF16)
        inv[:, span] = jnp.where(grown > 1.0, 1.0 / grown, 0.0).astype(BF16)

        @pl.when(step < depth - 1)
        def _():
            z_arrival(step + 1).wait_recv()
            spread(step + 1)

        @pl.when((step >= LAG) & (step < depth + LAG))
        def _():
            handed(step - LAG)

        @pl.when((step >= 2 * LAG) & (step < depth + 2 * LAG))
        def _():
            relayed(step - 2 * LAG)

    wide = QUARTERS * count
    slot = me * count + lax.rem(iota((wide, docs_total), 0), count)
    lane = iota((wide, docs_total), 1)
    order = jnp.zeros((wide, docs_total), jnp.int32)
    for r in range(slots.shape[0]):
        order = order + jnp.where(slots[r : r + 1, :] == slot, lane + r * docs_total, 0)
    order = jnp.sum(order.astype(F32), axis=1, keepdims=True)
    upto = (iota((docs_total, docs_total), 0) <= iota((docs_total, docs_total), 1)).astype(F32).astype(BF16)
    amount = jnp.broadcast_to(counts[...].astype(F32), (8, docs_total))
    ends = dot(amount.astype(BF16), upto, NN)[:1]
    begins = ends - amount[:1]
    member = ((order >= begins) & (order < ends)).astype(F32).astype(BF16)
    diagonal = iota((count, count), 0) == iota((count, count), 1)
    weight_column = jnp.sum(jnp.where(diagonal, weights[...], 0.0), axis=1, keepdims=True)
    weight_column = jnp.concatenate([weight_column] * QUARTERS, axis=0)
    diagonal = iota((wide, wide), 0) == iota((wide, wide), 1)
    weight_row = jnp.sum(jnp.where(diagonal, weight_column, 0.0), axis=0, keepdims=True)
    stacked = qx.shape[0] * qx.shape[1]
    per = qx.shape[1]
    each = per // QUARTERS
    one, two = iota((docs_total, stacked), 0), iota((docs_total, stacked), 1)
    select = (lax.div(one, each) == lax.div(two, per)) & (lax.rem(one, each) == lax.rem(two, each))
    select = select.astype(F32).astype(BF16)

    for k in range(steps - 2 * LAG, depth):
        relayed(k)

    @pl.loop(0, depth)
    def _(k):
        for j in range(ROWS):
            c_arrival(k, j).wait_recv()

    queries = qx[...].reshape(stacked, quarter)
    reps = jnp.concatenate([rep[:, i * quarter : (i + 1) * quarter] for i in range(QUARTERS)], axis=0)
    pair = dot(queries, reps, NT)
    row, column = iota((stacked, wide), 0), iota((stacked, wide), 1)
    pair = jnp.where(
        lax.rem(lax.div(row, each), QUARTERS) == lax.div(column, count), pair * weight_row, 0.0
    )
    high, low = halves(pair)
    paired = dot(select, high, NN) + dot(select, low, NN)
    high, low = halves(paired)
    parts[...] = dot(high, member, NN) + dot(low, member, NN)

    def group_peer(k):
        return (place(z, y, lax.rem(k, CORES)), lax.div(k, CORES))

    def rows_of(k):
        return pl.ds(pl.multiple_of(k * share, share), share)

    def a_copy(k):
        to = g_at(k)
        return remote(parts.at[rows_of(to)], box_a.at[g], a_send.at[k], a_recv.at[g], group_peer(to))

    def a_arrival(k):
        frm = g_at(k)
        return remote(box_a.at[frm], box_a.at[frm], a_send.at[k], a_recv.at[frm], group_peer(frm))

    for k in range(1, group):
        a_copy(k).start()
    box_a[g] = parts[rows_of(g), :]
    for k in range(1, group):
        a_arrival(k).wait_recv()
    box_b[y] = jnp.sum(box_a[...], axis=0)

    def b_copy(k):
        return remote(
            box_b.at[y], box_b.at[y], b_send.at[k], b_recv.at[y], (place(z, y_at(k), core), x)
        )

    def b_arrival(k):
        frm = y_at(k)
        return remote(
            box_b.at[frm], box_b.at[frm], b_send.at[k], b_recv.at[frm], (place(z, frm, core), x)
        )

    for k in range(1, ROWS):
        b_copy(k).start()
    for k in range(1, ROWS):
        b_arrival(k).wait_recv()
    box_c[z] = jnp.sum(box_b[...], axis=0)

    def d_copy(k):
        return remote(
            box_c.at[z], box_c.at[z], d_send.at[k], d_recv.at[z], (place(z_at(k), y, core), x)
        )

    def d_arrival(k):
        frm = z_at(k)
        return remote(
            box_c.at[frm], box_c.at[frm], d_send.at[k], d_recv.at[frm], (place(frm, y, core), x)
        )

    for k in range(1, depth):
        d_copy(k).start()
    for k in range(1, depth):
        d_arrival(k).wait_recv()
    scores[rows_of(g), :] = jnp.sum(box_c[...], axis=0)

    def e_copy(k):
        mine = scores.at[rows_of(g)]
        return remote(mine, mine, e_send.at[k], e_recv.at[g], group_peer(g_at(k)))

    def e_arrival(k):
        frm = g_at(k)
        theirs = scores.at[rows_of(frm)]
        return remote(theirs, theirs, e_send.at[k], e_recv.at[frm], group_peer(frm))

    for k in range(1, group):
        e_copy(k).start()
    for k in range(1, group):
        e_arrival(k).wait_recv()

    score = scores[...]
    shape = (docs_total, docs_total)
    owned = scores_out.shape[0]
    for r in range(owned):
        scores_out[r : r + 1, :] = jnp.sum(
            jnp.where(iota(shape, 0) == me * owned + r, score, 0.0), axis=0, keepdims=True
        )
    power = jnp.exp(score - jnp.max(score, axis=1, keepdims=True))
    prob = power / jnp.sum(power, axis=1, keepdims=True)
    dscore = (prob - (iota(shape, 0) == iota(shape, 1)).astype(F32)) / docs_total

    high, low = halves(dscore)
    per_query = (dot(member, high, NT) + dot(member, low, NT)) * weight_column
    high, low = halves(per_query)
    spread_out = dot(jnp.concatenate([high, low], axis=0), select, NN)
    row, column = iota((2 * wide, stacked), 0), iota((2 * wide, stacked), 1)
    keep = lax.rem(lax.div(row, count), QUARTERS) == lax.rem(lax.div(column, each), QUARTERS)
    spread_out = jnp.where(keep, spread_out, 0.0).astype(BF16)
    cut = 5 * 128

    @pl.loop(0, quarter // cut)
    def _(i):
        span = pl.ds(pl.multiple_of(i * cut, cut), cut)
        found = dot(spread_out, qx[:, :, span].reshape(stacked, cut), NN)
        found = found[:wide] + found[wide:]
        for part in range(QUARTERS):
            there = pl.ds(pl.multiple_of(part * quarter + i * cut, 128), cut)
            value = found[part * count : (part + 1) * count].astype(BF16)
            for t in range(picks):
                lines = slice(t * count, (t + 1) * count)
                inv[lines, there] = inv[lines, there] * value

    def block_rows(k):
        return pl.ds(pl.multiple_of(k * piece_rows, piece_rows), piece_rows)

    def x_peer(k):
        return (me, k)

    def r_copy(j, k):
        to = x_at(k)
        return remote(
            part_send.at[j, block_rows(to)],
            part_box.at[j, x],
            r_send.at[j, k],
            r_recv.at[j, x],
            x_peer(to),
        )

    def r_arrival(j, k):
        frm = x_at(k)
        spot = part_box.at[j, frm]
        return remote(spot, spot, r_send.at[j, k], r_recv.at[j, frm], x_peer(frm))

    def t_copy(j, k):
        mine = total.at[j, block_rows(x)]
        return remote(mine, mine, g_send.at[j, k], g_recv.at[j, x], x_peer(x_at(k)))

    def t_arrival(j, k):
        frm = x_at(k)
        theirs = total.at[j, block_rows(frm)]
        return remote(theirs, theirs, g_send.at[j, k], g_recv.at[j, frm], x_peer(frm))

    def finish(j):
        value = part_own[j, block_rows(x), :]
        for k in range(1, blocks):
            r_arrival(j, k).wait_recv()
            value = value + part_box[j, x_at(k)].astype(F32)
        total[j, block_rows(x), :] = value.astype(BF16)
        for k in range(1, blocks):
            t_copy(j, k).start()

    @pl.loop(0, lots)
    def _(j):
        span = pl.ds(pl.multiple_of(j * columns, columns), columns)
        value = dot(inv[...], w[span, :], NT)
        part_own[j] = value
        part_send[j] = value.astype(BF16)
        for k in range(1, blocks):
            r_copy(j, k).start()

    for j in range(lots):
        finish(j)

    @pl.loop(0, lots)
    def _(j):
        for k in range(1, blocks):
            t_arrival(j, k).wait_recv()

    @pl.loop(1, depth)
    def _(k):
        z_copy(k).wait_send()

    @pl.loop(0, depth)
    def _(k):
        for j in range(2):
            y_copy(k, j).wait_send()
            h_copy(k, j).wait_send()
        for j in range(ROWS):
            c_copy(k, j).wait_send()

    for k in range(1, group):
        a_copy(k).wait_send()
        e_copy(k).wait_send()
    for k in range(1, ROWS):
        b_copy(k).wait_send()
    for k in range(1, depth):
        d_copy(k).wait_send()

    @pl.loop(0, lots)
    def _(j):
        for k in range(1, blocks):
            r_copy(j, k).wait_send()
            t_copy(j, k).wait_send()


def solution(mesh):
    passes, blocks = mesh.shape["pass"], mesh.shape["voc"]
    depth = passes // (ROWS * CORES)
    group = blocks * CORES

    def on_device(
        hidden, positions, passage_weight, passage_counts, passage_slot, head_weight, head_bias, queries
    ):
        count, length, width = hidden.shape
        picks = positions.shape[1]
        tokens = count * picks
        docs = passage_counts.shape[0]
        vocab = head_weight.shape[1]
        owned = queries.shape[0]
        quarter = vocab // QUARTERS
        per = QUARTERS * owned
        share = docs // group
        columns = width // 3
        lots = 3
        piece = queries.reshape(owned, QUARTERS, quarter).transpose(1, 0, 2)
        vmem = pl.BlockSpec(memory_space=pltpu.VMEM)
        anywhere = pl.BlockSpec(memory_space=pl.ANY)
        dma = pltpu.SemaphoreType.DMA
        scores, sums, hits = pl.pallas_call(
            functools.partial(kernel, depth, blocks),
            out_shape=(
                pltpu.VMEM((owned, docs), F32),
                pltpu.VMEM((lots, tokens, columns), BF16),
                pltpu.VMEM((count * length, tokens), BF16),
            ),
            in_specs=[anywhere] * 8,
            out_specs=(vmem, vmem, vmem),
            scratch_shapes=[
                pltpu.VMEM((width, vocab), BF16),
                pltpu.VMEM((tokens, vocab), BF16),
                pltpu.VMEM((count, vocab), BF16),
                pltpu.VMEM((per, quarter), BF16),
                pltpu.VMEM((passes, per, quarter), BF16),
                pltpu.VMEM((tokens, width), BF16),
                pltpu.VMEM((docs, docs), F32),
                pltpu.VMEM((group, share, docs), F32),
                pltpu.VMEM((ROWS, share, docs), F32),
                pltpu.VMEM((depth, share, docs), F32),
                pltpu.VMEM((docs, docs), F32),
                pltpu.VMEM((lots, tokens, columns), F32),
                pltpu.VMEM((lots, tokens, columns), BF16),
                pltpu.VMEM((lots, blocks, tokens // blocks, columns), BF16),
                pltpu.VMEM((count * length, width), BF16),
                pltpu.VMEM((picks, count), jnp.int32),
                pltpu.VMEM((1, count), F32),
                pltpu.VMEM((1, docs), jnp.int32),
                pltpu.VMEM((passage_slot.shape[0] // docs, docs), jnp.int32),
                pltpu.VMEM((vocab // 128, 128), F32),
                pltpu.VMEM((QUARTERS, owned, quarter), BF16),
                dma((7,)),
                dma((vocab // FORWARD,)),
                dma,
                dma((depth,)),
                dma((depth,)),
                dma((depth, 2)),
                dma((depth, 2)),
                dma((depth, 2)),
                dma((depth, 2)),
                dma((depth, ROWS)),
                dma((depth, ROWS)),
                dma((group,)),
                dma((group,)),
                dma((ROWS,)),
                dma((ROWS,)),
                dma((depth,)),
                dma((depth,)),
                dma((group,)),
                dma((group,)),
                dma((lots, blocks)),
                dma((lots, blocks)),
                dma((lots, blocks)),
                dma((lots, blocks)),
            ],
            compiler_params=pltpu.CompilerParams(collective_id=0, has_side_effects=True),
        )(
            hidden.reshape(count * length, width),
            positions.T,
            passage_weight.reshape(1, count),
            passage_counts.reshape(1, docs),
            passage_slot.reshape(-1, docs),
            head_weight,
            head_bias.reshape(vocab // 128, 128),
            piece,
        )
        grad, scores = pl.pallas_call(
            expand,
            out_shape=(
                jax.ShapeDtypeStruct((count * length, width), BF16),
                jax.ShapeDtypeStruct((owned, docs), F32),
            ),
            in_specs=[vmem] * 3,
            out_specs=(anywhere, vmem),
            scratch_shapes=[pltpu.VMEM((4, count * length // 4, width), BF16), dma((4,))],
        )(*(pltpu.with_memory_space_constraint(kept, pltpu.VMEM) for kept in (hits, sums, scores)))
        return scores, grad.reshape(count, length, width)

    placed = (
        P("pass", None, None),
        P("pass", None),
        P("pass"),
        P(),
        P(),
        P(None, "voc"),
        P("voc"),
        P("pass", "voc"),
    )
    return jax.shard_map(
        on_device,
        mesh=mesh,
        in_specs=placed,
        out_specs=(P("pass", None), P("pass", None, None)),
        check_vma=False,
    )
```

```python
import functools

import jax
import jax.numpy as jnp
from jax import lax
from jax.experimental import pallas as pl
from jax.experimental.pallas import tpu as pltpu
from jax.sharding import PartitionSpec as P

MESH = pl.DeviceIdType.MESH
CORES = 2
ROWS = 4
QUARTERS = 4
FORWARD = 512
LAG = 7
AWAY = (1, 3)
HALF = (pl.ds(0, 1024), pl.ds(1024, 896))
F32 = jnp.float32
BF16 = jnp.bfloat16
NT = (((1,), (1,)), ((), ()))
NN = (((1,), (0,)), ((), ()))
TN = (((0,), (0,)), ((), ()))


def dot(a, b, dims):
    return lax.dot_general(a, b, dims, preferred_element_type=F32)


def halves(a):
    high = a.astype(BF16)
    return high, (a - high.astype(F32)).astype(BF16)


def iota(shape, dim):
    return lax.broadcasted_iota(jnp.int32, shape, dim)


def token_hits(positions, rows):
    picks, count = positions.shape
    tokens = picks * count
    passage = (iota((count, tokens), 0) == lax.rem(iota((count, tokens), 1), count)).astype(F32)
    spread = dot(positions[...].astype(F32).astype(BF16), passage.astype(BF16), NN)
    own = iota((picks, tokens), 0) == lax.div(iota((picks, tokens), 1), count)
    chosen = jnp.sum(jnp.where(own, spread, 0.0), axis=0, keepdims=True).astype(jnp.int32)
    length = rows // count
    goal = chosen + length * lax.rem(iota((1, tokens), 1), count)
    return (iota((rows, tokens), 0) == goal).astype(F32).astype(BF16)


def expand(hits, sums, scores, grad_hbm, scores_out, grad, out_sem):
    scores_out[...] = scores[...]
    pieces, rows, _ = grad.shape
    columns = sums.shape[2]
    stores = []
    for i in range(pieces):
        lines = slice(i * rows, (i + 1) * rows)
        for j in range(sums.shape[0]):
            grad[i, :, j * columns : (j + 1) * columns] = dot(hits[lines, :], sums[j], NN).astype(BF16)
        store = pltpu.make_async_copy(grad.at[i], grad_hbm.at[pl.ds(i * rows, rows)], out_sem.at[i])
        store.start()
        stores.append(store)
    for store in stores:
        store.wait()


def kernel(
    depth,
    blocks,
    hidden_hbm,
    positions_hbm,
    weights_hbm,
    counts_hbm,
    slots_hbm,
    w_hbm,
    bias_hbm,
    q_hbm,
    scores_out,
    total,
    hits,
    w,
    inv,
    rep,
    piece,
    qx,
    picked,
    parts,
    box_a,
    box_b,
    box_c,
    scores,
    part_own,
    part_send,
    part_box,
    hidden,
    positions,
    weights,
    counts,
    slots,
    bias,
    q_own,
    in_sem,
    w_sem,
    q_sem,
    z_send,
    z_recv,
    y_send,
    y_recv,
    h_send,
    h_recv,
    c_send,
    c_recv,
    a_send,
    a_recv,
    b_send,
    b_recv,
    d_send,
    d_recv,
    e_send,
    e_recv,
    r_send,
    r_recv,
    g_send,
    g_recv,
):
    me = lax.axis_index("pass")
    x = lax.axis_index("voc")
    core = lax.rem(me, CORES)
    y = lax.rem(lax.div(me, CORES), ROWS)
    z = lax.div(me, CORES * ROWS)
    group = blocks * CORES
    g = x * CORES + core
    vocab = w.shape[1]
    width = w.shape[0]
    count = rep.shape[0]
    picks = picked.shape[0] // count
    docs_total = counts.shape[1]
    quarter = vocab // QUARTERS
    share = docs_total // group
    steps = vocab // FORWARD
    columns = width // 3
    tokens = picked.shape[0]
    lots = part_own.shape[0]
    piece_rows = tokens // blocks

    def place(zz, yy, cc):
        return (zz * ROWS + yy) * CORES + cc

    def z_at(k):
        return lax.rem(z + k, depth)

    def y_at(k):
        return lax.rem(y + k, ROWS)

    def x_at(k):
        return lax.rem(x + k, blocks)

    def g_at(k):
        return lax.rem(g + k, group)

    def distance(k):
        odd = lax.rem(k, 2)
        return odd * lax.div(k + 1, 2) + (1 - odd) * lax.rem(depth - lax.div(k, 2), depth)

    other = 1 - core

    barrier = pltpu.get_barrier_semaphore()
    peers = [(place(z_at(k), y, core), x) for k in range(1, depth)]
    peers += [(place(z, y_at(k), core), x) for k in range(1, ROWS)]
    peers += [(place(z, y, lax.rem(g_at(k), CORES)), lax.div(g_at(k), CORES)) for k in range(1, group)]
    for peer in peers:
        pl.semaphore_signal(barrier, inc=1, device_id=peer, device_id_type=MESH)

    small = [
        pltpu.make_async_copy(src, dst, in_sem.at[i])
        for i, (src, dst) in enumerate(
            (
                (q_hbm, q_own),
                (positions_hbm, positions),
                (hidden_hbm, hidden),
                (weights_hbm, weights),
                (counts_hbm, counts),
                (slots_hbm, slots),
                (bias_hbm, bias),
            )
        )
    ]
    for copy in small:
        copy.start()

    def w_copy(step):
        span = pl.ds(pl.multiple_of(step * FORWARD, FORWARD), FORWARD)
        return pltpu.make_async_copy(w_hbm.at[:, span], w.at[:, span], w_sem.at[step])

    @pl.loop(0, steps)
    def _(step):
        w_copy(step).start()

    small[0].wait()
    piece[...] = jnp.concatenate([q_own[i] for i in range(QUARTERS)], axis=0)
    q_copy = pltpu.make_async_copy(piece, qx.at[me], q_sem)
    q_copy.start()

    q_copy.wait()
    pl.semaphore_wait(barrier, len(peers))

    def remote(src, dst, send, recv, peer):
        return pltpu.make_async_remote_copy(
            src_ref=src, dst_ref=dst, send_sem=send, recv_sem=recv, device_id=peer, device_id_type=MESH
        )

    def z_copy(k):
        return remote(
            qx.at[me],
            qx.at[me],
            z_send.at[k],
            z_recv.at[k],
            (place(z_at(distance(k)), y, core), x),
        )

    def from_z(k):
        return z_at(depth - distance(k))

    def z_arrival(k):
        spot = qx.at[place(from_z(k), y, core)]
        return remote(spot, spot, z_send.at[k], z_recv.at[k], (place(from_z(k), y, core), x))

    def y_copy(k, j):
        spot = qx.at[place(from_z(k), y, core)]
        return remote(spot, spot, y_send.at[k, j], y_recv.at[k, j], (place(z, y_at(AWAY[j]), core), x))

    def y_arrival(k, j):
        frm = y_at(ROWS - AWAY[j])
        spot = qx.at[place(from_z(k), frm, core)]
        return remote(spot, spot, y_send.at[k, j], y_recv.at[k, j], (place(z, frm, core), x))

    def h_copy(k, j):
        spot = qx.at[place(from_z(k), y_at(ROWS - AWAY[j]), core), :, HALF[j]]
        return remote(spot, spot, h_send.at[k, j], h_recv.at[k, j], (place(z, y_at(AWAY[j]), core), x))

    def h_arrival(k, j):
        spot = qx.at[place(from_z(k), y_at(2), core), :, HALF[j]]
        frm = y_at(ROWS - AWAY[j])
        return remote(spot, spot, h_send.at[k, j], h_recv.at[k, j], (place(z, frm, core), x))

    def c_copy(k, j):
        spot = qx.at[place(from_z(k), y_at(j), core)]
        return remote(spot, spot, c_send.at[k, j], c_recv.at[k, j], (place(z, y, other), x))

    def c_arrival(k, j):
        spot = qx.at[place(from_z(k), y_at(j), other)]
        return remote(spot, spot, c_send.at[k, j], c_recv.at[k, j], (place(z, y, other), x))

    def spread(k):
        for j in range(2):
            y_copy(k, j).start()
        c_copy(k, 0).start()

    def handed(k):
        for j in range(2):
            y_arrival(k, j).wait_recv()
            h_copy(k, j).start()
            c_copy(k, ROWS - AWAY[j]).start()

    def relayed(k):
        for j in range(2):
            h_arrival(k, j).wait_recv()
        c_copy(k, 2).start()

    @pl.loop(1, depth)
    def _(k):
        z_copy(k).start()

    spread(0)

    for copy in small[1:]:
        copy.wait()
    hit = token_hits(positions, hidden.shape[0])
    hits[...] = hit
    picked[...] = dot(hit, hidden[...], TN).astype(BF16)

    @pl.loop(0, steps)
    def _(step):
        w_copy(step).wait()
        span = pl.ds(pl.multiple_of(step * FORWARD, FORWARD), FORWARD)
        lines = FORWARD // 128
        offset = jnp.concatenate([bias[pl.ds(step * lines + i, 1), :] for i in range(lines)], axis=1) + 1.0
        grown = jnp.maximum(dot(picked[...], w[:, span], NN) + offset, 1.0)
        product = grown[:count]
        for t in range(1, picks):
            product = product * grown[t * count : (t + 1) * count]
        rep[:, span] = jnp.log(product).astype(BF16)
        inv[:, span] = jnp.where(grown > 1.0, 1.0 / grown, 0.0).astype(BF16)

        @pl.when(step < depth - 1)
        def _():
            z_arrival(step + 1).wait_recv()
            spread(step + 1)

        @pl.when((step >= LAG) & (step < depth + LAG))
        def _():
            handed(step - LAG)

        @pl.when((step >= 2 * LAG) & (step < depth + 2 * LAG))
        def _():
            relayed(step - 2 * LAG)

    wide = QUARTERS * count
    slot = me * count + lax.rem(iota((wide, docs_total), 0), count)
    lane = iota((wide, docs_total), 1)
    order = jnp.zeros((wide, docs_total), jnp.int32)
    for r in range(slots.shape[0]):
        order = order + jnp.where(slots[r : r + 1, :] == slot, lane + r * docs_total, 0)
    order = jnp.sum(order.astype(F32), axis=1, keepdims=True)
    upto = (iota((docs_total, docs_total), 0) <= iota((docs_total, docs_total), 1)).astype(F32).astype(BF16)
    amount = jnp.broadcast_to(counts[...].astype(F32), (8, docs_total))
    ends = dot(amount.astype(BF16), upto, NN)[:1]
    begins = ends - amount[:1]
    member = ((order >= begins) & (order < ends)).astype(F32).astype(BF16)
    diagonal = iota((count, count), 0) == iota((count, count), 1)
    weight_column = jnp.sum(jnp.where(diagonal, weights[...], 0.0), axis=1, keepdims=True)
    weight_column = jnp.concatenate([weight_column] * QUARTERS, axis=0)
    diagonal = iota((wide, wide), 0) == iota((wide, wide), 1)
    weight_row = jnp.sum(jnp.where(diagonal, weight_column, 0.0), axis=0, keepdims=True)
    stacked = qx.shape[0] * qx.shape[1]
    per = qx.shape[1]
    each = per // QUARTERS
    one, two = iota((docs_total, stacked), 0), iota((docs_total, stacked), 1)
    select = (lax.div(one, each) == lax.div(two, per)) & (lax.rem(one, each) == lax.rem(two, each))
    select = select.astype(F32).astype(BF16)

    for k in range(steps - 2 * LAG, depth):
        relayed(k)

    @pl.loop(0, depth)
    def _(k):
        for j in range(ROWS):
            c_arrival(k, j).wait_recv()

    queries = qx[...].reshape(stacked, quarter)
    reps = jnp.concatenate([rep[:, i * quarter : (i + 1) * quarter] for i in range(QUARTERS)], axis=0)
    pair = dot(queries, reps, NT)
    row, column = iota((stacked, wide), 0), iota((stacked, wide), 1)
    pair = jnp.where(
        lax.rem(lax.div(row, each), QUARTERS) == lax.div(column, count), pair * weight_row, 0.0
    )
    high, low = halves(pair)
    paired = dot(select, high, NN) + dot(select, low, NN)
    high, low = halves(paired)
    parts[...] = dot(high, member, NN) + dot(low, member, NN)

    def group_peer(k):
        return (place(z, y, lax.rem(k, CORES)), lax.div(k, CORES))

    def rows_of(k):
        return pl.ds(pl.multiple_of(k * share, share), share)

    def a_copy(k):
        to = g_at(k)
        return remote(parts.at[rows_of(to)], box_a.at[g], a_send.at[k], a_recv.at[g], group_peer(to))

    def a_arrival(k):
        frm = g_at(k)
        return remote(box_a.at[frm], box_a.at[frm], a_send.at[k], a_recv.at[frm], group_peer(frm))

    for k in range(1, group):
        a_copy(k).start()
    box_a[g] = parts[rows_of(g), :]
    for k in range(1, group):
        a_arrival(k).wait_recv()
    box_b[y] = jnp.sum(box_a[...], axis=0)

    def b_copy(k):
        return remote(
            box_b.at[y], box_b.at[y], b_send.at[k], b_recv.at[y], (place(z, y_at(k), core), x)
        )

    def b_arrival(k):
        frm = y_at(k)
        return remote(
            box_b.at[frm], box_b.at[frm], b_send.at[k], b_recv.at[frm], (place(z, frm, core), x)
        )

    for k in range(1, ROWS):
        b_copy(k).start()
    for k in range(1, ROWS):
        b_arrival(k).wait_recv()
    box_c[z] = jnp.sum(box_b[...], axis=0)

    def d_copy(k):
        return remote(
            box_c.at[z], box_c.at[z], d_send.at[k], d_recv.at[z], (place(z_at(k), y, core), x)
        )

    def d_arrival(k):
        frm = z_at(k)
        return remote(
            box_c.at[frm], box_c.at[frm], d_send.at[k], d_recv.at[frm], (place(frm, y, core), x)
        )

    for k in range(1, depth):
        d_copy(k).start()
    for k in range(1, depth):
        d_arrival(k).wait_recv()
    scores[rows_of(g), :] = jnp.sum(box_c[...], axis=0)

    def e_copy(k):
        mine = scores.at[rows_of(g)]
        return remote(mine, mine, e_send.at[k], e_recv.at[g], group_peer(g_at(k)))

    def e_arrival(k):
        frm = g_at(k)
        theirs = scores.at[rows_of(frm)]
        return remote(theirs, theirs, e_send.at[k], e_recv.at[frm], group_peer(frm))

    for k in range(1, group):
        e_copy(k).start()
    for k in range(1, group):
        e_arrival(k).wait_recv()

    score = scores[...]
    shape = (docs_total, docs_total)
    owned = scores_out.shape[0]
    for r in range(owned):
        scores_out[r : r + 1, :] = jnp.sum(
            jnp.where(iota(shape, 0) == me * owned + r, score, 0.0), axis=0, keepdims=True
        )
    power = jnp.exp(score - jnp.max(score, axis=1, keepdims=True))
    prob = power / jnp.sum(power, axis=1, keepdims=True)
    dscore = (prob - (iota(shape, 0) == iota(shape, 1)).astype(F32)) / docs_total

    high, low = halves(dscore)
    per_query = (dot(member, high, NT) + dot(member, low, NT)) * weight_column
    high, low = halves(per_query)
    spread_out = dot(jnp.concatenate([high, low], axis=0), select, NN)
    row, column = iota((2 * wide, stacked), 0), iota((2 * wide, stacked), 1)
    keep = lax.rem(lax.div(row, count), QUARTERS) == lax.rem(lax.div(column, each), QUARTERS)
    spread_out = jnp.where(keep, spread_out, 0.0).astype(BF16)
    cut = 5 * 128

    @pl.loop(0, quarter // cut)
    def _(i):
        span = pl.ds(pl.multiple_of(i * cut, cut), cut)
        found = dot(spread_out, qx[:, :, span].reshape(stacked, cut), NN)
        found = found[:wide] + found[wide:]
        for part in range(QUARTERS):
            there = pl.ds(pl.multiple_of(part * quarter + i * cut, 128), cut)
            value = found[part * count : (part + 1) * count].astype(BF16)
            for t in range(picks):
                lines = slice(t * count, (t + 1) * count)
                inv[lines, there] = inv[lines, there] * value

    def block_rows(k):
        return pl.ds(pl.multiple_of(k * piece_rows, piece_rows), piece_rows)

    def x_peer(k):
        return (me, k)

    def r_copy(j, k):
        to = x_at(k)
        return remote(
            part_send.at[j, block_rows(to)],
            part_box.at[j, x],
            r_send.at[j, k],
            r_recv.at[j, x],
            x_peer(to),
        )

    def r_arrival(j, k):
        frm = x_at(k)
        spot = part_box.at[j, frm]
        return remote(spot, spot, r_send.at[j, k], r_recv.at[j, frm], x_peer(frm))

    def t_copy(j, k):
        mine = total.at[j, block_rows(x)]
        return remote(mine, mine, g_send.at[j, k], g_recv.at[j, x], x_peer(x_at(k)))

    def t_arrival(j, k):
        frm = x_at(k)
        theirs = total.at[j, block_rows(frm)]
        return remote(theirs, theirs, g_send.at[j, k], g_recv.at[j, frm], x_peer(frm))

    def finish(j):
        value = part_own[j, block_rows(x), :]
        for k in range(1, blocks):
            r_arrival(j, k).wait_recv()
            value = value + part_box[j, x_at(k)].astype(F32)
        total[j, block_rows(x), :] = value.astype(BF16)
        for k in range(1, blocks):
            t_copy(j, k).start()

    @pl.loop(0, lots)
    def _(j):
        span = pl.ds(pl.multiple_of(j * columns, columns), columns)
        value = dot(inv[...], w[span, :], NT)
        part_own[j] = value
        part_send[j] = value.astype(BF16)
        for k in range(1, blocks):
            r_copy(j, k).start()

    for j in range(lots):
        finish(j)

    @pl.loop(0, lots)
    def _(j):
        for k in range(1, blocks):
            t_arrival(j, k).wait_recv()

    @pl.loop(1, depth)
    def _(k):
        z_copy(k).wait_send()

    @pl.loop(0, depth)
    def _(k):
        for j in range(2):
            y_copy(k, j).wait_send()
            h_copy(k, j).wait_send()
        for j in range(ROWS):
            c_copy(k, j).wait_send()

    for k in range(1, group):
        a_copy(k).wait_send()
        e_copy(k).wait_send()
    for k in range(1, ROWS):
        b_copy(k).wait_send()
    for k in range(1, depth):
        d_copy(k).wait_send()

    @pl.loop(0, lots)
    def _(j):
        for k in range(1, blocks):
            r_copy(j, k).wait_send()
            t_copy(j, k).wait_send()


def solution(mesh):
    passes, blocks = mesh.shape["pass"], mesh.shape["voc"]
    depth = passes // (ROWS * CORES)
    group = blocks * CORES

    def on_device(
        hidden, positions, passage_weight, passage_counts, passage_slot, head_weight, head_bias, queries
    ):
        count, length, width = hidden.shape
        picks = positions.shape[1]
        tokens = count * picks
        docs = passage_counts.shape[0]
        vocab = head_weight.shape[1]
        owned = queries.shape[0]
        quarter = vocab // QUARTERS
        per = QUARTERS * owned
        share = docs // group
        columns = width // 3
        lots = 3
        piece = queries.reshape(owned, QUARTERS, quarter).transpose(1, 0, 2)
        vmem = pl.BlockSpec(memory_space=pltpu.VMEM)
        anywhere = pl.BlockSpec(memory_space=pl.ANY)
        dma = pltpu.SemaphoreType.DMA
        scores, sums, hits = pl.pallas_call(
            functools.partial(kernel, depth, blocks),
            out_shape=(
                pltpu.VMEM((owned, docs), F32),
                pltpu.VMEM((lots, tokens, columns), BF16),
                pltpu.VMEM((count * length, tokens), BF16),
            ),
            in_specs=[anywhere] * 8,
            out_specs=(vmem, vmem, vmem),
            scratch_shapes=[
                pltpu.VMEM((width, vocab), BF16),
                pltpu.VMEM((tokens, vocab), BF16),
                pltpu.VMEM((count, vocab), BF16),
                pltpu.VMEM((per, quarter), BF16),
                pltpu.VMEM((passes, per, quarter), BF16),
                pltpu.VMEM((tokens, width), BF16),
                pltpu.VMEM((docs, docs), F32),
                pltpu.VMEM((group, share, docs), F32),
                pltpu.VMEM((ROWS, share, docs), F32),
                pltpu.VMEM((depth, share, docs), F32),
                pltpu.VMEM((docs, docs), F32),
                pltpu.VMEM((lots, tokens, columns), F32),
                pltpu.VMEM((lots, tokens, columns), BF16),
                pltpu.VMEM((lots, blocks, tokens // blocks, columns), BF16),
                pltpu.VMEM((count * length, width), BF16),
                pltpu.VMEM((picks, count), jnp.int32),
                pltpu.VMEM((1, count), F32),
                pltpu.VMEM((1, docs), jnp.int32),
                pltpu.VMEM((passage_slot.shape[0] // docs, docs), jnp.int32),
                pltpu.VMEM((vocab // 128, 128), F32),
                pltpu.VMEM((QUARTERS, owned, quarter), BF16),
                dma((7,)),
                dma((vocab // FORWARD,)),
                dma,
                dma((depth,)),
                dma((depth,)),
                dma((depth, 2)),
                dma((depth, 2)),
                dma((depth, 2)),
                dma((depth, 2)),
                dma((depth, ROWS)),
                dma((depth, ROWS)),
                dma((group,)),
                dma((group,)),
                dma((ROWS,)),
                dma((ROWS,)),
                dma((depth,)),
                dma((depth,)),
                dma((group,)),
                dma((group,)),
                dma((lots, blocks)),
                dma((lots, blocks)),
                dma((lots, blocks)),
                dma((lots, blocks)),
            ],
            compiler_params=pltpu.CompilerParams(collective_id=0, has_side_effects=True),
        )(
            hidden.reshape(count * length, width),
            positions.T,
            passage_weight.reshape(1, count),
            passage_counts.reshape(1, docs),
            passage_slot.reshape(-1, docs),
            head_weight,
            head_bias.reshape(vocab // 128, 128),
            piece,
        )
        grad, scores = pl.pallas_call(
            expand,
            out_shape=(
                jax.ShapeDtypeStruct((count * length, width), BF16),
                jax.ShapeDtypeStruct((owned, docs), F32),
            ),
            in_specs=[vmem] * 3,
            out_specs=(anywhere, vmem),
            scratch_shapes=[pltpu.VMEM((4, count * length // 4, width), BF16), dma((4,))],
        )(*(pltpu.with_memory_space_constraint(kept, pltpu.VMEM) for kept in (hits, sums, scores)))
        return scores, grad.reshape(count, length, width)

    placed = (
        P("pass", None, None),
        P("pass", None),
        P("pass"),
        P(),
        P(),
        P(None, "voc"),
        P("voc"),
        P("pass", "voc"),
    )
    return jax.shard_map(
        on_device,
        mesh=mesh,
        in_specs=placed,
        out_specs=(P("pass", None), P("pass", None, None)),
        check_vma=False,
    )
```

```python
import functools

import jax
import jax.numpy as jnp
from jax import lax
from jax.experimental import pallas as pl
from jax.experimental.pallas import tpu as pltpu
from jax.sharding import PartitionSpec as P

MESH = pl.DeviceIdType.MESH
CORES = 2
ROWS = 4
QUARTERS = 4
FORWARD = 512
LAG = 7
AWAY = (1, 3, 2)
FAR = 4
HALF = (pl.ds(0, 1024), pl.ds(1024, 896))
F32 = jnp.float32
BF16 = jnp.bfloat16
NT = (((1,), (1,)), ((), ()))
NN = (((1,), (0,)), ((), ()))
TN = (((0,), (0,)), ((), ()))


def dot(a, b, dims):
    return lax.dot_general(a, b, dims, preferred_element_type=F32)


def halves(a):
    high = a.astype(BF16)
    return high, (a - high.astype(F32)).astype(BF16)


def iota(shape, dim):
    return lax.broadcasted_iota(jnp.int32, shape, dim)


def token_hits(positions, rows):
    picks, count = positions.shape
    tokens = picks * count
    passage = (iota((count, tokens), 0) == lax.rem(iota((count, tokens), 1), count)).astype(F32)
    spread = dot(positions[...].astype(F32).astype(BF16), passage.astype(BF16), NN)
    own = iota((picks, tokens), 0) == lax.div(iota((picks, tokens), 1), count)
    chosen = jnp.sum(jnp.where(own, spread, 0.0), axis=0, keepdims=True).astype(jnp.int32)
    length = rows // count
    goal = chosen + length * lax.rem(iota((1, tokens), 1), count)
    return (iota((rows, tokens), 0) == goal).astype(F32).astype(BF16)


def expand(hits, sums, scores, grad_hbm, scores_out, grad, out_sem):
    scores_out[...] = scores[...]
    pieces, rows, _ = grad.shape
    columns = sums.shape[2]
    stores = []
    for i in range(pieces):
        lines = slice(i * rows, (i + 1) * rows)
        for j in range(sums.shape[0]):
            grad[i, :, j * columns : (j + 1) * columns] = dot(hits[lines, :], sums[j], NN).astype(BF16)
        store = pltpu.make_async_copy(grad.at[i], grad_hbm.at[pl.ds(i * rows, rows)], out_sem.at[i])
        store.start()
        stores.append(store)
    for store in stores:
        store.wait()


def kernel(
    depth,
    blocks,
    hidden_hbm,
    positions_hbm,
    weights_hbm,
    counts_hbm,
    slots_hbm,
    w_hbm,
    bias_hbm,
    q_hbm,
    scores_out,
    total,
    hits,
    w,
    inv,
    rep,
    piece,
    qx,
    picked,
    parts,
    box_a,
    box_b,
    box_c,
    scores,
    part_own,
    part_send,
    part_box,
    hidden,
    positions,
    weights,
    counts,
    slots,
    bias,
    q_own,
    in_sem,
    w_sem,
    q_sem,
    z_send,
    z_recv,
    y_send,
    y_recv,
    h_send,
    h_recv,
    c_send,
    c_recv,
    a_send,
    a_recv,
    b_send,
    b_recv,
    d_send,
    d_recv,
    e_send,
    e_recv,
    r_send,
    r_recv,
    g_send,
    g_recv,
):
    me = lax.axis_index("pass")
    x = lax.axis_index("voc")
    core = lax.rem(me, CORES)
    y = lax.rem(lax.div(me, CORES), ROWS)
    z = lax.div(me, CORES * ROWS)
    group = blocks * CORES
    g = x * CORES + core
    vocab = w.shape[1]
    width = w.shape[0]
    count = rep.shape[0]
    picks = picked.shape[0] // count
    docs_total = counts.shape[1]
    quarter = vocab // QUARTERS
    share = docs_total // group
    steps = vocab // FORWARD
    columns = width // 3
    tokens = picked.shape[0]
    lots = part_own.shape[0]
    piece_rows = tokens // blocks

    def place(zz, yy, cc):
        return (zz * ROWS + yy) * CORES + cc

    def z_at(k):
        return lax.rem(z + k, depth)

    def y_at(k):
        return lax.rem(y + k, ROWS)

    def x_at(k):
        return lax.rem(x + k, blocks)

    def g_at(k):
        return lax.rem(g + k, group)

    def distance(k):
        odd = lax.rem(k, 2)
        return odd * lax.div(k + 1, 2) + (1 - odd) * lax.rem(depth - lax.div(k, 2), depth)

    other = 1 - core

    barrier = pltpu.get_barrier_semaphore()
    peers = [(place(z_at(k), y, core), x) for k in range(1, depth)]
    peers += [(place(z, y_at(k), core), x) for k in range(1, ROWS)]
    peers += [(place(z, y, lax.rem(g_at(k), CORES)), lax.div(g_at(k), CORES)) for k in range(1, group)]
    for peer in peers:
        pl.semaphore_signal(barrier, inc=1, device_id=peer, device_id_type=MESH)

    small = [
        pltpu.make_async_copy(src, dst, in_sem.at[i])
        for i, (src, dst) in enumerate(
            (
                (q_hbm, q_own),
                (positions_hbm, positions),
                (hidden_hbm, hidden),
                (weights_hbm, weights),
                (counts_hbm, counts),
                (slots_hbm, slots),
                (bias_hbm, bias),
            )
        )
    ]
    for copy in small:
        copy.start()

    def w_copy(step):
        span = pl.ds(pl.multiple_of(step * FORWARD, FORWARD), FORWARD)
        return pltpu.make_async_copy(w_hbm.at[:, span], w.at[:, span], w_sem.at[step])

    @pl.loop(0, steps)
    def _(step):
        w_copy(step).start()

    small[0].wait()
    piece[...] = jnp.concatenate([q_own[i] for i in range(QUARTERS)], axis=0)
    q_copy = pltpu.make_async_copy(piece, qx.at[me], q_sem)
    q_copy.start()

    q_copy.wait()
    pl.semaphore_wait(barrier, len(peers))

    def remote(src, dst, send, recv, peer):
        return pltpu.make_async_remote_copy(
            src_ref=src, dst_ref=dst, send_sem=send, recv_sem=recv, device_id=peer, device_id_type=MESH
        )

    def z_copy(k):
        return remote(
            qx.at[me],
            qx.at[me],
            z_send.at[k],
            z_recv.at[k],
            (place(z_at(distance(k)), y, core), x),
        )

    def from_z(k):
        return z_at(depth - distance(k))

    def z_arrival(k):
        spot = qx.at[place(from_z(k), y, core)]
        return remote(spot, spot, z_send.at[k], z_recv.at[k], (place(from_z(k), y, core), x))

    def y_copy(k, j):
        spot = qx.at[place(from_z(k), y, core)]
        return remote(spot, spot, y_send.at[k, j], y_recv.at[k, j], (place(z, y_at(AWAY[j]), core), x))

    def y_arrival(k, j):
        frm = y_at(ROWS - AWAY[j])
        spot = qx.at[place(from_z(k), frm, core)]
        return remote(spot, spot, y_send.at[k, j], y_recv.at[k, j], (place(z, frm, core), x))

    def h_copy(k, j):
        spot = qx.at[place(from_z(k), y_at(ROWS - AWAY[j]), core), :, HALF[j]]
        return remote(spot, spot, h_send.at[k, j], h_recv.at[k, j], (place(z, y_at(AWAY[j]), core), x))

    def h_arrival(k, j):
        spot = qx.at[place(from_z(k), y_at(2), core), :, HALF[j]]
        frm = y_at(ROWS - AWAY[j])
        return remote(spot, spot, h_send.at[k, j], h_recv.at[k, j], (place(z, frm, core), x))

    def c_copy(k, j):
        spot = qx.at[place(from_z(k), y_at(j), core)]
        return remote(spot, spot, c_send.at[k, j], c_recv.at[k, j], (place(z, y, other), x))

    def c_arrival(k, j):
        spot = qx.at[place(from_z(k), y_at(j), other)]
        return remote(spot, spot, c_send.at[k, j], c_recv.at[k, j], (place(z, y, other), x))

    def spread(k):
        for j in range(2):
            y_copy(k, j).start()

        @pl.when(k >= FAR)
        def _():
            y_copy(k, 2).start()

        c_copy(k, 0).start()

    def handed(k):
        for j in range(2):
            y_arrival(k, j).wait_recv()

            @pl.when(k < FAR)
            def _():
                h_copy(k, j).start()

            c_copy(k, ROWS - AWAY[j]).start()

    def relayed(k):
        @pl.when(k < FAR)
        def _():
            for j in range(2):
                h_arrival(k, j).wait_recv()

        @pl.when(k >= FAR)
        def _():
            y_arrival(k, 2).wait_recv()

        c_copy(k, 2).start()

    @pl.loop(1, depth)
    def _(k):
        z_copy(k).start()

    spread(jnp.int32(0))

    for copy in small[1:]:
        copy.wait()
    hit = token_hits(positions, hidden.shape[0])
    hits[...] = hit
    picked[...] = dot(hit, hidden[...], TN).astype(BF16)

    @pl.loop(0, steps)
    def _(step):
        w_copy(step).wait()
        span = pl.ds(pl.multiple_of(step * FORWARD, FORWARD), FORWARD)
        lines = FORWARD // 128
        offset = jnp.concatenate([bias[pl.ds(step * lines + i, 1), :] for i in range(lines)], axis=1) + 1.0
        grown = jnp.maximum(dot(picked[...], w[:, span], NN) + offset, 1.0)
        product = grown[:count]
        for t in range(1, picks):
            product = product * grown[t * count : (t + 1) * count]
        rep[:, span] = jnp.log(product).astype(BF16)
        inv[:, span] = jnp.where(grown > 1.0, 1.0 / grown, 0.0).astype(BF16)

        @pl.when(step < depth - 1)
        def _():
            z_arrival(step + 1).wait_recv()
            spread(step + 1)

        @pl.when((step >= LAG) & (step < depth + LAG))
        def _():
            handed(step - LAG)

        @pl.when((step >= 2 * LAG) & (step < depth + 2 * LAG))
        def _():
            relayed(step - 2 * LAG)

    wide = QUARTERS * count
    slot = me * count + lax.rem(iota((wide, docs_total), 0), count)
    lane = iota((wide, docs_total), 1)
    order = jnp.zeros((wide, docs_total), jnp.int32)
    for r in range(slots.shape[0]):
        order = order + jnp.where(slots[r : r + 1, :] == slot, lane + r * docs_total, 0)
    order = jnp.sum(order.astype(F32), axis=1, keepdims=True)
    upto = (iota((docs_total, docs_total), 0) <= iota((docs_total, docs_total), 1)).astype(F32).astype(BF16)
    amount = jnp.broadcast_to(counts[...].astype(F32), (8, docs_total))
    ends = dot(amount.astype(BF16), upto, NN)[:1]
    begins = ends - amount[:1]
    member = ((order >= begins) & (order < ends)).astype(F32).astype(BF16)
    diagonal = iota((count, count), 0) == iota((count, count), 1)
    weight_column = jnp.sum(jnp.where(diagonal, weights[...], 0.0), axis=1, keepdims=True)
    weight_column = jnp.concatenate([weight_column] * QUARTERS, axis=0)
    diagonal = iota((wide, wide), 0) == iota((wide, wide), 1)
    weight_row = jnp.sum(jnp.where(diagonal, weight_column, 0.0), axis=0, keepdims=True)
    stacked = qx.shape[0] * qx.shape[1]
    per = qx.shape[1]
    each = per // QUARTERS
    one, two = iota((docs_total, stacked), 0), iota((docs_total, stacked), 1)
    select = (lax.div(one, each) == lax.div(two, per)) & (lax.rem(one, each) == lax.rem(two, each))
    select = select.astype(F32).astype(BF16)

    @pl.loop(steps - 2 * LAG, depth)
    def _(k):
        relayed(k)

    @pl.loop(0, depth)
    def _(k):
        for j in range(ROWS):
            c_arrival(k, j).wait_recv()

    queries = qx[...].reshape(stacked, quarter)
    reps = jnp.concatenate([rep[:, i * quarter : (i + 1) * quarter] for i in range(QUARTERS)], axis=0)
    pair = dot(queries, reps, NT)
    row, column = iota((stacked, wide), 0), iota((stacked, wide), 1)
    pair = jnp.where(
        lax.rem(lax.div(row, each), QUARTERS) == lax.div(column, count), pair * weight_row, 0.0
    )
    high, low = halves(pair)
    paired = dot(select, high, NN) + dot(select, low, NN)
    high, low = halves(paired)
    parts[...] = dot(high, member, NN) + dot(low, member, NN)

    def group_peer(k):
        return (place(z, y, lax.rem(k, CORES)), lax.div(k, CORES))

    def rows_of(k):
        return pl.ds(pl.multiple_of(k * share, share), share)

    def a_copy(k):
        to = g_at(k)
        return remote(parts.at[rows_of(to)], box_a.at[g], a_send.at[k], a_recv.at[g], group_peer(to))

    def a_arrival(k):
        frm = g_at(k)
        return remote(box_a.at[frm], box_a.at[frm], a_send.at[k], a_recv.at[frm], group_peer(frm))

    for k in range(1, group):
        a_copy(k).start()
    box_a[g] = parts[rows_of(g), :]

    @pl.loop(1, depth)
    def _(k):
        z_copy(k).wait_send()

    @pl.loop(0, depth)
    def _(k):
        for j in range(2):
            y_copy(k, j).wait_send()

            @pl.when(k < FAR)
            def _():
                h_copy(k, j).wait_send()

        @pl.when(k >= FAR)
        def _():
            y_copy(k, 2).wait_send()

        for j in range(ROWS):
            c_copy(k, j).wait_send()

    for k in range(1, group):
        a_arrival(k).wait_recv()
    box_b[y] = jnp.sum(box_a[...], axis=0)

    def b_copy(k):
        return remote(
            box_b.at[y], box_b.at[y], b_send.at[k], b_recv.at[y], (place(z, y_at(k), core), x)
        )

    def b_arrival(k):
        frm = y_at(k)
        return remote(
            box_b.at[frm], box_b.at[frm], b_send.at[k], b_recv.at[frm], (place(z, frm, core), x)
        )

    for k in range(1, ROWS):
        b_copy(k).start()
    for k in range(1, ROWS):
        b_arrival(k).wait_recv()
    box_c[z] = jnp.sum(box_b[...], axis=0)

    def d_copy(k):
        return remote(
            box_c.at[z], box_c.at[z], d_send.at[k], d_recv.at[z], (place(z_at(k), y, core), x)
        )

    def d_arrival(k):
        frm = z_at(k)
        return remote(
            box_c.at[frm], box_c.at[frm], d_send.at[k], d_recv.at[frm], (place(frm, y, core), x)
        )

    for k in range(1, depth):
        d_copy(k).start()
    for k in range(1, depth):
        d_arrival(k).wait_recv()
    scores[rows_of(g), :] = jnp.sum(box_c[...], axis=0)

    def e_copy(k):
        mine = scores.at[rows_of(g)]
        return remote(mine, mine, e_send.at[k], e_recv.at[g], group_peer(g_at(k)))

    def e_arrival(k):
        frm = g_at(k)
        theirs = scores.at[rows_of(frm)]
        return remote(theirs, theirs, e_send.at[k], e_recv.at[frm], group_peer(frm))

    for k in range(1, group):
        e_copy(k).start()
    for k in range(1, group):
        e_arrival(k).wait_recv()

    score = scores[...]
    shape = (docs_total, docs_total)
    owned = scores_out.shape[0]
    for r in range(owned):
        scores_out[r : r + 1, :] = jnp.sum(
            jnp.where(iota(shape, 0) == me * owned + r, score, 0.0), axis=0, keepdims=True
        )
    power = jnp.exp(score - jnp.max(score, axis=1, keepdims=True))
    prob = power / jnp.sum(power, axis=1, keepdims=True)
    dscore = (prob - (iota(shape, 0) == iota(shape, 1)).astype(F32)) / docs_total

    high, low = halves(dscore)
    per_query = (dot(member, high, NT) + dot(member, low, NT)) * weight_column
    high, low = halves(per_query)
    spread_out = dot(jnp.concatenate([high, low], axis=0), select, NN)
    row, column = iota((2 * wide, stacked), 0), iota((2 * wide, stacked), 1)
    keep = lax.rem(lax.div(row, count), QUARTERS) == lax.rem(lax.div(column, each), QUARTERS)
    spread_out = jnp.where(keep, spread_out, 0.0).astype(BF16)
    cut = 5 * 128

    @pl.loop(0, quarter // cut)
    def _(i):
        span = pl.ds(pl.multiple_of(i * cut, cut), cut)
        found = dot(spread_out, qx[:, :, span].reshape(stacked, cut), NN)
        found = found[:wide] + found[wide:]
        for part in range(QUARTERS):
            there = pl.ds(pl.multiple_of(part * quarter + i * cut, 128), cut)
            value = found[part * count : (part + 1) * count].astype(BF16)
            for t in range(picks):
                lines = slice(t * count, (t + 1) * count)
                inv[lines, there] = inv[lines, there] * value

    def block_rows(k):
        return pl.ds(pl.multiple_of(k * piece_rows, piece_rows), piece_rows)

    def x_peer(k):
        return (me, k)

    def r_copy(j, k):
        to = x_at(k)
        return remote(
            part_send.at[j, block_rows(to)],
            part_box.at[j, x],
            r_send.at[j, k],
            r_recv.at[j, x],
            x_peer(to),
        )

    def r_arrival(j, k):
        frm = x_at(k)
        spot = part_box.at[j, frm]
        return remote(spot, spot, r_send.at[j, k], r_recv.at[j, frm], x_peer(frm))

    def t_copy(j, k):
        mine = total.at[j, block_rows(x)]
        return remote(mine, mine, g_send.at[j, k], g_recv.at[j, x], x_peer(x_at(k)))

    def t_arrival(j, k):
        frm = x_at(k)
        theirs = total.at[j, block_rows(frm)]
        return remote(theirs, theirs, g_send.at[j, k], g_recv.at[j, frm], x_peer(frm))

    def finish(j):
        value = part_own[j, block_rows(x), :]
        for k in range(1, blocks):
            r_arrival(j, k).wait_recv()
            value = value + part_box[j, x_at(k)].astype(F32)
        total[j, block_rows(x), :] = value.astype(BF16)
        for k in range(1, blocks):
            t_copy(j, k).start()

    @pl.loop(0, lots)
    def _(j):
        span = pl.ds(pl.multiple_of(j * columns, columns), columns)
        value = dot(inv[...], w[span, :], NT)
        part_own[j] = value
        part_send[j] = value.astype(BF16)
        for k in range(1, blocks):
            r_copy(j, k).start()

    for j in range(lots):
        finish(j)

    @pl.loop(0, lots)
    def _(j):
        for k in range(1, blocks):
            t_arrival(j, k).wait_recv()

    for k in range(1, group):
        a_copy(k).wait_send()
        e_copy(k).wait_send()
    for k in range(1, ROWS):
        b_copy(k).wait_send()
    for k in range(1, depth):
        d_copy(k).wait_send()

    @pl.loop(0, lots)
    def _(j):
        for k in range(1, blocks):
            r_copy(j, k).wait_send()
            t_copy(j, k).wait_send()


def solution(mesh):
    passes, blocks = mesh.shape["pass"], mesh.shape["voc"]
    depth = passes // (ROWS * CORES)
    group = blocks * CORES

    def on_device(
        hidden, positions, passage_weight, passage_counts, passage_slot, head_weight, head_bias, queries
    ):
        count, length, width = hidden.shape
        picks = positions.shape[1]
        tokens = count * picks
        docs = passage_counts.shape[0]
        vocab = head_weight.shape[1]
        owned = queries.shape[0]
        quarter = vocab // QUARTERS
        per = QUARTERS * owned
        share = docs // group
        columns = width // 3
        lots = 3
        piece = queries.reshape(owned, QUARTERS, quarter).transpose(1, 0, 2)
        vmem = pl.BlockSpec(memory_space=pltpu.VMEM)
        anywhere = pl.BlockSpec(memory_space=pl.ANY)
        dma = pltpu.SemaphoreType.DMA
        scores, sums, hits = pl.pallas_call(
            functools.partial(kernel, depth, blocks),
            out_shape=(
                pltpu.VMEM((owned, docs), F32),
                pltpu.VMEM((lots, tokens, columns), BF16),
                pltpu.VMEM((count * length, tokens), BF16),
            ),
            in_specs=[anywhere] * 8,
            out_specs=(vmem, vmem, vmem),
            scratch_shapes=[
                pltpu.VMEM((width, vocab), BF16),
                pltpu.VMEM((tokens, vocab), BF16),
                pltpu.VMEM((count, vocab), BF16),
                pltpu.VMEM((per, quarter), BF16),
                pltpu.VMEM((passes, per, quarter), BF16),
                pltpu.VMEM((tokens, width), BF16),
                pltpu.VMEM((docs, docs), F32),
                pltpu.VMEM((group, share, docs), F32),
                pltpu.VMEM((ROWS, share, docs), F32),
                pltpu.VMEM((depth, share, docs), F32),
                pltpu.VMEM((docs, docs), F32),
                pltpu.VMEM((lots, tokens, columns), F32),
                pltpu.VMEM((lots, tokens, columns), BF16),
                pltpu.VMEM((lots, blocks, tokens // blocks, columns), BF16),
                pltpu.VMEM((count * length, width), BF16),
                pltpu.VMEM((picks, count), jnp.int32),
                pltpu.VMEM((1, count), F32),
                pltpu.VMEM((1, docs), jnp.int32),
                pltpu.VMEM((passage_slot.shape[0] // docs, docs), jnp.int32),
                pltpu.VMEM((vocab // 128, 128), F32),
                pltpu.VMEM((QUARTERS, owned, quarter), BF16),
                dma((7,)),
                dma((vocab // FORWARD,)),
                dma,
                dma((depth,)),
                dma((depth,)),
                dma((depth, 3)),
                dma((depth, 3)),
                dma((depth, 2)),
                dma((depth, 2)),
                dma((depth, ROWS)),
                dma((depth, ROWS)),
                dma((group,)),
                dma((group,)),
                dma((ROWS,)),
                dma((ROWS,)),
                dma((depth,)),
                dma((depth,)),
                dma((group,)),
                dma((group,)),
                dma((lots, blocks)),
                dma((lots, blocks)),
                dma((lots, blocks)),
                dma((lots, blocks)),
            ],
            compiler_params=pltpu.CompilerParams(collective_id=0, has_side_effects=True),
        )(
            hidden.reshape(count * length, width),
            positions.T,
            passage_weight.reshape(1, count),
            passage_counts.reshape(1, docs),
            passage_slot.reshape(-1, docs),
            head_weight,
            head_bias.reshape(vocab // 128, 128),
            piece,
        )
        grad, scores = pl.pallas_call(
            expand,
            out_shape=(
                jax.ShapeDtypeStruct((count * length, width), BF16),
                jax.ShapeDtypeStruct((owned, docs), F32),
            ),
            in_specs=[vmem] * 3,
            out_specs=(anywhere, vmem),
            scratch_shapes=[pltpu.VMEM((4, count * length // 4, width), BF16), dma((4,))],
        )(*(pltpu.with_memory_space_constraint(kept, pltpu.VMEM) for kept in (hits, sums, scores)))
        return scores, grad.reshape(count, length, width)

    placed = (
        P("pass", None, None),
        P("pass", None),
        P("pass"),
        P(),
        P(),
        P(None, "voc"),
        P("voc"),
        P("pass", "voc"),
    )
    return jax.shard_map(
        on_device,
        mesh=mesh,
        in_specs=placed,
        out_specs=(P("pass", None), P("pass", None, None)),
        check_vma=False,
    )
```

```python
import functools

import jax
import jax.numpy as jnp
from jax import lax
from jax.experimental import pallas as pl
from jax.experimental.pallas import tpu as pltpu
from jax.sharding import PartitionSpec as P

MESH = pl.DeviceIdType.MESH
CORES = 2
ROWS = 4
QUARTERS = 4
FORWARD = 512
LAG = 7
AWAY = (1, 3, 2)
FAR = 0
HALF = (pl.ds(0, 1024), pl.ds(1024, 896))
F32 = jnp.float32
BF16 = jnp.bfloat16
NT = (((1,), (1,)), ((), ()))
NN = (((1,), (0,)), ((), ()))
TN = (((0,), (0,)), ((), ()))


def dot(a, b, dims):
    return lax.dot_general(a, b, dims, preferred_element_type=F32)


def halves(a):
    high = a.astype(BF16)
    return high, (a - high.astype(F32)).astype(BF16)


def iota(shape, dim):
    return lax.broadcasted_iota(jnp.int32, shape, dim)


def token_hits(positions, rows):
    picks, count = positions.shape
    tokens = picks * count
    passage = (iota((count, tokens), 0) == lax.rem(iota((count, tokens), 1), count)).astype(F32)
    spread = dot(positions[...].astype(F32).astype(BF16), passage.astype(BF16), NN)
    own = iota((picks, tokens), 0) == lax.div(iota((picks, tokens), 1), count)
    chosen = jnp.sum(jnp.where(own, spread, 0.0), axis=0, keepdims=True).astype(jnp.int32)
    length = rows // count
    goal = chosen + length * lax.rem(iota((1, tokens), 1), count)
    return (iota((rows, tokens), 0) == goal).astype(F32).astype(BF16)


def expand(hits, sums, scores, grad_hbm, scores_out, grad, out_sem):
    scores_out[...] = scores[...]
    pieces, rows, _ = grad.shape
    columns = sums.shape[2]
    stores = []
    for i in range(pieces):
        lines = slice(i * rows, (i + 1) * rows)
        for j in range(sums.shape[0]):
            grad[i, :, j * columns : (j + 1) * columns] = dot(hits[lines, :], sums[j], NN).astype(BF16)
        store = pltpu.make_async_copy(grad.at[i], grad_hbm.at[pl.ds(i * rows, rows)], out_sem.at[i])
        store.start()
        stores.append(store)
    for store in stores:
        store.wait()


def kernel(
    depth,
    blocks,
    hidden_hbm,
    positions_hbm,
    weights_hbm,
    counts_hbm,
    slots_hbm,
    w_hbm,
    bias_hbm,
    q_hbm,
    scores_out,
    total,
    hits,
    w,
    inv,
    rep,
    piece,
    qx,
    picked,
    parts,
    box_a,
    box_b,
    box_c,
    scores,
    part_own,
    part_send,
    part_box,
    hidden,
    positions,
    weights,
    counts,
    slots,
    bias,
    q_own,
    in_sem,
    w_sem,
    q_sem,
    z_send,
    z_recv,
    y_send,
    y_recv,
    h_send,
    h_recv,
    c_send,
    c_recv,
    a_send,
    a_recv,
    b_send,
    b_recv,
    d_send,
    d_recv,
    e_send,
    e_recv,
    r_send,
    r_recv,
    g_send,
    g_recv,
):
    me = lax.axis_index("pass")
    x = lax.axis_index("voc")
    core = lax.rem(me, CORES)
    y = lax.rem(lax.div(me, CORES), ROWS)
    z = lax.div(me, CORES * ROWS)
    group = blocks * CORES
    g = x * CORES + core
    vocab = w.shape[1]
    width = w.shape[0]
    count = rep.shape[0]
    picks = picked.shape[0] // count
    docs_total = counts.shape[1]
    quarter = vocab // QUARTERS
    share = docs_total // group
    steps = vocab // FORWARD
    columns = width // 3
    tokens = picked.shape[0]
    lots = part_own.shape[0]
    piece_rows = tokens // blocks

    def place(zz, yy, cc):
        return (zz * ROWS + yy) * CORES + cc

    def z_at(k):
        return lax.rem(z + k, depth)

    def y_at(k):
        return lax.rem(y + k, ROWS)

    def x_at(k):
        return lax.rem(x + k, blocks)

    def g_at(k):
        return lax.rem(g + k, group)

    def distance(k):
        odd = lax.rem(k, 2)
        return odd * lax.div(k + 1, 2) + (1 - odd) * lax.rem(depth - lax.div(k, 2), depth)

    other = 1 - core

    barrier = pltpu.get_barrier_semaphore()
    peers = [(place(z_at(k), y, core), x) for k in range(1, depth)]
    peers += [(place(z, y_at(k), core), x) for k in range(1, ROWS)]
    peers += [(place(z, y, lax.rem(g_at(k), CORES)), lax.div(g_at(k), CORES)) for k in range(1, group)]
    for peer in peers:
        pl.semaphore_signal(barrier, inc=1, device_id=peer, device_id_type=MESH)

    small = [
        pltpu.make_async_copy(src, dst, in_sem.at[i])
        for i, (src, dst) in enumerate(
            (
                (q_hbm, q_own),
                (positions_hbm, positions),
                (hidden_hbm, hidden),
                (weights_hbm, weights),
                (counts_hbm, counts),
                (slots_hbm, slots),
                (bias_hbm, bias),
            )
        )
    ]
    for copy in small:
        copy.start()

    def w_copy(step):
        span = pl.ds(pl.multiple_of(step * FORWARD, FORWARD), FORWARD)
        return pltpu.make_async_copy(w_hbm.at[:, span], w.at[:, span], w_sem.at[step])

    @pl.loop(0, steps)
    def _(step):
        w_copy(step).start()

    small[0].wait()
    piece[...] = jnp.concatenate([q_own[i] for i in range(QUARTERS)], axis=0)
    q_copy = pltpu.make_async_copy(piece, qx.at[me], q_sem)
    q_copy.start()

    q_copy.wait()
    pl.semaphore_wait(barrier, len(peers))

    def remote(src, dst, send, recv, peer):
        return pltpu.make_async_remote_copy(
            src_ref=src, dst_ref=dst, send_sem=send, recv_sem=recv, device_id=peer, device_id_type=MESH
        )

    def z_copy(k):
        return remote(
            qx.at[me],
            qx.at[me],
            z_send.at[k],
            z_recv.at[k],
            (place(z_at(distance(k)), y, core), x),
        )

    def from_z(k):
        return z_at(depth - distance(k))

    def z_arrival(k):
        spot = qx.at[place(from_z(k), y, core)]
        return remote(spot, spot, z_send.at[k], z_recv.at[k], (place(from_z(k), y, core), x))

    def y_copy(k, j):
        spot = qx.at[place(from_z(k), y, core)]
        return remote(spot, spot, y_send.at[k, j], y_recv.at[k, j], (place(z, y_at(AWAY[j]), core), x))

    def y_arrival(k, j):
        frm = y_at(ROWS - AWAY[j])
        spot = qx.at[place(from_z(k), frm, core)]
        return remote(spot, spot, y_send.at[k, j], y_recv.at[k, j], (place(z, frm, core), x))

    def h_copy(k, j):
        spot = qx.at[place(from_z(k), y_at(ROWS - AWAY[j]), core), :, HALF[j]]
        return remote(spot, spot, h_send.at[k, j], h_recv.at[k, j], (place(z, y_at(AWAY[j]), core), x))

    def h_arrival(k, j):
        spot = qx.at[place(from_z(k), y_at(2), core), :, HALF[j]]
        frm = y_at(ROWS - AWAY[j])
        return remote(spot, spot, h_send.at[k, j], h_recv.at[k, j], (place(z, frm, core), x))

    def c_copy(k, j):
        spot = qx.at[place(from_z(k), y_at(j), core)]
        return remote(spot, spot, c_send.at[k, j], c_recv.at[k, j], (place(z, y, other), x))

    def c_arrival(k, j):
        spot = qx.at[place(from_z(k), y_at(j), other)]
        return remote(spot, spot, c_send.at[k, j], c_recv.at[k, j], (place(z, y, other), x))

    def spread(k):
        for j in range(2):
            y_copy(k, j).start()

        @pl.when(k >= FAR)
        def _():
            y_copy(k, 2).start()

        c_copy(k, 0).start()

    def handed(k):
        for j in range(2):
            y_arrival(k, j).wait_recv()

            @pl.when(k < FAR)
            def _():
                h_copy(k, j).start()

            c_copy(k, ROWS - AWAY[j]).start()

    def relayed(k):
        @pl.when(k < FAR)
        def _():
            for j in range(2):
                h_arrival(k, j).wait_recv()

        @pl.when(k >= FAR)
        def _():
            y_arrival(k, 2).wait_recv()

        c_copy(k, 2).start()

    @pl.loop(1, depth)
    def _(k):
        z_copy(k).start()

    spread(jnp.int32(0))

    for copy in small[1:]:
        copy.wait()
    hit = token_hits(positions, hidden.shape[0])
    hits[...] = hit
    picked[...] = dot(hit, hidden[...], TN).astype(BF16)

    @pl.loop(0, steps)
    def _(step):
        w_copy(step).wait()
        span = pl.ds(pl.multiple_of(step * FORWARD, FORWARD), FORWARD)
        lines = FORWARD // 128
        offset = jnp.concatenate([bias[pl.ds(step * lines + i, 1), :] for i in range(lines)], axis=1) + 1.0
        grown = jnp.maximum(dot(picked[...], w[:, span], NN) + offset, 1.0)
        product = grown[:count]
        for t in range(1, picks):
            product = product * grown[t * count : (t + 1) * count]
        rep[:, span] = jnp.log(product).astype(BF16)
        inv[:, span] = jnp.where(grown > 1.0, 1.0 / grown, 0.0).astype(BF16)

        @pl.when(step < depth - 1)
        def _():
            z_arrival(step + 1).wait_recv()
            spread(step + 1)

        @pl.when((step >= LAG) & (step < depth + LAG))
        def _():
            handed(step - LAG)

        @pl.when((step >= 2 * LAG) & (step < depth + 2 * LAG))
        def _():
            relayed(step - 2 * LAG)

    wide = QUARTERS * count
    slot = me * count + lax.rem(iota((wide, docs_total), 0), count)
    lane = iota((wide, docs_total), 1)
    order = jnp.zeros((wide, docs_total), jnp.int32)
    for r in range(slots.shape[0]):
        order = order + jnp.where(slots[r : r + 1, :] == slot, lane + r * docs_total, 0)
    order = jnp.sum(order.astype(F32), axis=1, keepdims=True)
    upto = (iota((docs_total, docs_total), 0) <= iota((docs_total, docs_total), 1)).astype(F32).astype(BF16)
    amount = jnp.broadcast_to(counts[...].astype(F32), (8, docs_total))
    ends = dot(amount.astype(BF16), upto, NN)[:1]
    begins = ends - amount[:1]
    member = ((order >= begins) & (order < ends)).astype(F32).astype(BF16)
    diagonal = iota((count, count), 0) == iota((count, count), 1)
    weight_column = jnp.sum(jnp.where(diagonal, weights[...], 0.0), axis=1, keepdims=True)
    weight_column = jnp.concatenate([weight_column] * QUARTERS, axis=0)
    diagonal = iota((wide, wide), 0) == iota((wide, wide), 1)
    weight_row = jnp.sum(jnp.where(diagonal, weight_column, 0.0), axis=0, keepdims=True)
    stacked = qx.shape[0] * qx.shape[1]
    per = qx.shape[1]
    each = per // QUARTERS
    one, two = iota((docs_total, stacked), 0), iota((docs_total, stacked), 1)
    select = (lax.div(one, each) == lax.div(two, per)) & (lax.rem(one, each) == lax.rem(two, each))
    select = select.astype(F32).astype(BF16)

    @pl.loop(steps - 2 * LAG, depth)
    def _(k):
        relayed(k)

    @pl.loop(0, depth)
    def _(k):
        for j in range(ROWS):
            c_arrival(k, j).wait_recv()

    queries = qx[...].reshape(stacked, quarter)
    reps = jnp.concatenate([rep[:, i * quarter : (i + 1) * quarter] for i in range(QUARTERS)], axis=0)
    pair = dot(queries, reps, NT)
    row, column = iota((stacked, wide), 0), iota((stacked, wide), 1)
    pair = jnp.where(
        lax.rem(lax.div(row, each), QUARTERS) == lax.div(column, count), pair * weight_row, 0.0
    )
    high, low = halves(pair)
    paired = dot(select, high, NN) + dot(select, low, NN)
    high, low = halves(paired)
    parts[...] = dot(high, member, NN) + dot(low, member, NN)

    def group_peer(k):
        return (place(z, y, lax.rem(k, CORES)), lax.div(k, CORES))

    def rows_of(k):
        return pl.ds(pl.multiple_of(k * share, share), share)

    def a_copy(k):
        to = g_at(k)
        return remote(parts.at[rows_of(to)], box_a.at[g], a_send.at[k], a_recv.at[g], group_peer(to))

    def a_arrival(k):
        frm = g_at(k)
        return remote(box_a.at[frm], box_a.at[frm], a_send.at[k], a_recv.at[frm], group_peer(frm))

    for k in range(1, group):
        a_copy(k).start()
    box_a[g] = parts[rows_of(g), :]

    @pl.loop(1, depth)
    def _(k):
        z_copy(k).wait_send()

    @pl.loop(0, depth)
    def _(k):
        for j in range(2):
            y_copy(k, j).wait_send()

            @pl.when(k < FAR)
            def _():
                h_copy(k, j).wait_send()

        @pl.when(k >= FAR)
        def _():
            y_copy(k, 2).wait_send()

        for j in range(ROWS):
            c_copy(k, j).wait_send()

    for k in range(1, group):
        a_arrival(k).wait_recv()
    box_b[y] = jnp.sum(box_a[...], axis=0)

    def b_copy(k):
        return remote(
            box_b.at[y], box_b.at[y], b_send.at[k], b_recv.at[y], (place(z, y_at(k), core), x)
        )

    def b_arrival(k):
        frm = y_at(k)
        return remote(
            box_b.at[frm], box_b.at[frm], b_send.at[k], b_recv.at[frm], (place(z, frm, core), x)
        )

    for k in range(1, ROWS):
        b_copy(k).start()
    for k in range(1, ROWS):
        b_arrival(k).wait_recv()
    box_c[z] = jnp.sum(box_b[...], axis=0)

    def d_copy(k):
        return remote(
            box_c.at[z], box_c.at[z], d_send.at[k], d_recv.at[z], (place(z_at(k), y, core), x)
        )

    def d_arrival(k):
        frm = z_at(k)
        return remote(
            box_c.at[frm], box_c.at[frm], d_send.at[k], d_recv.at[frm], (place(frm, y, core), x)
        )

    for k in range(1, depth):
        d_copy(k).start()
    for k in range(1, depth):
        d_arrival(k).wait_recv()
    scores[rows_of(g), :] = jnp.sum(box_c[...], axis=0)

    def e_copy(k):
        mine = scores.at[rows_of(g)]
        return remote(mine, mine, e_send.at[k], e_recv.at[g], group_peer(g_at(k)))

    def e_arrival(k):
        frm = g_at(k)
        theirs = scores.at[rows_of(frm)]
        return remote(theirs, theirs, e_send.at[k], e_recv.at[frm], group_peer(frm))

    for k in range(1, group):
        e_copy(k).start()
    for k in range(1, group):
        e_arrival(k).wait_recv()

    score = scores[...]
    shape = (docs_total, docs_total)
    owned = scores_out.shape[0]
    for r in range(owned):
        scores_out[r : r + 1, :] = jnp.sum(
            jnp.where(iota(shape, 0) == me * owned + r, score, 0.0), axis=0, keepdims=True
        )
    power = jnp.exp(score - jnp.max(score, axis=1, keepdims=True))
    prob = power / jnp.sum(power, axis=1, keepdims=True)
    dscore = (prob - (iota(shape, 0) == iota(shape, 1)).astype(F32)) / docs_total

    high, low = halves(dscore)
    per_query = (dot(member, high, NT) + dot(member, low, NT)) * weight_column
    high, low = halves(per_query)
    spread_out = dot(jnp.concatenate([high, low], axis=0), select, NN)
    row, column = iota((2 * wide, stacked), 0), iota((2 * wide, stacked), 1)
    keep = lax.rem(lax.div(row, count), QUARTERS) == lax.rem(lax.div(column, each), QUARTERS)
    spread_out = jnp.where(keep, spread_out, 0.0).astype(BF16)
    cut = 5 * 128

    @pl.loop(0, quarter // cut)
    def _(i):
        span = pl.ds(pl.multiple_of(i * cut, cut), cut)
        found = dot(spread_out, qx[:, :, span].reshape(stacked, cut), NN)
        found = found[:wide] + found[wide:]
        for part in range(QUARTERS):
            there = pl.ds(pl.multiple_of(part * quarter + i * cut, 128), cut)
            value = found[part * count : (part + 1) * count].astype(BF16)
            for t in range(picks):
                lines = slice(t * count, (t + 1) * count)
                inv[lines, there] = inv[lines, there] * value

    def block_rows(k):
        return pl.ds(pl.multiple_of(k * piece_rows, piece_rows), piece_rows)

    def x_peer(k):
        return (me, k)

    def r_copy(j, k):
        to = x_at(k)
        return remote(
            part_send.at[j, block_rows(to)],
            part_box.at[j, x],
            r_send.at[j, k],
            r_recv.at[j, x],
            x_peer(to),
        )

    def r_arrival(j, k):
        frm = x_at(k)
        spot = part_box.at[j, frm]
        return remote(spot, spot, r_send.at[j, k], r_recv.at[j, frm], x_peer(frm))

    def t_copy(j, k):
        mine = total.at[j, block_rows(x)]
        return remote(mine, mine, g_send.at[j, k], g_recv.at[j, x], x_peer(x_at(k)))

    def t_arrival(j, k):
        frm = x_at(k)
        theirs = total.at[j, block_rows(frm)]
        return remote(theirs, theirs, g_send.at[j, k], g_recv.at[j, frm], x_peer(frm))

    def finish(j):
        value = part_own[j, block_rows(x), :]
        for k in range(1, blocks):
            r_arrival(j, k).wait_recv()
            value = value + part_box[j, x_at(k)].astype(F32)
        total[j, block_rows(x), :] = value.astype(BF16)
        for k in range(1, blocks):
            t_copy(j, k).start()

    @pl.loop(0, lots)
    def _(j):
        span = pl.ds(pl.multiple_of(j * columns, columns), columns)
        value = dot(inv[...], w[span, :], NT)
        part_own[j] = value
        part_send[j] = value.astype(BF16)
        for k in range(1, blocks):
            r_copy(j, k).start()

    for j in range(lots):
        finish(j)

    @pl.loop(0, lots)
    def _(j):
        for k in range(1, blocks):
            t_arrival(j, k).wait_recv()

    for k in range(1, group):
        a_copy(k).wait_send()
        e_copy(k).wait_send()
    for k in range(1, ROWS):
        b_copy(k).wait_send()
    for k in range(1, depth):
        d_copy(k).wait_send()

    @pl.loop(0, lots)
    def _(j):
        for k in range(1, blocks):
            r_copy(j, k).wait_send()
            t_copy(j, k).wait_send()


def solution(mesh):
    passes, blocks = mesh.shape["pass"], mesh.shape["voc"]
    depth = passes // (ROWS * CORES)
    group = blocks * CORES

    def on_device(
        hidden, positions, passage_weight, passage_counts, passage_slot, head_weight, head_bias, queries
    ):
        count, length, width = hidden.shape
        picks = positions.shape[1]
        tokens = count * picks
        docs = passage_counts.shape[0]
        vocab = head_weight.shape[1]
        owned = queries.shape[0]
        quarter = vocab // QUARTERS
        per = QUARTERS * owned
        share = docs // group
        columns = width // 3
        lots = 3
        piece = queries.reshape(owned, QUARTERS, quarter).transpose(1, 0, 2)
        vmem = pl.BlockSpec(memory_space=pltpu.VMEM)
        anywhere = pl.BlockSpec(memory_space=pl.ANY)
        dma = pltpu.SemaphoreType.DMA
        scores, sums, hits = pl.pallas_call(
            functools.partial(kernel, depth, blocks),
            out_shape=(
                pltpu.VMEM((owned, docs), F32),
                pltpu.VMEM((lots, tokens, columns), BF16),
                pltpu.VMEM((count * length, tokens), BF16),
            ),
            in_specs=[anywhere] * 8,
            out_specs=(vmem, vmem, vmem),
            scratch_shapes=[
                pltpu.VMEM((width, vocab), BF16),
                pltpu.VMEM((tokens, vocab), BF16),
                pltpu.VMEM((count, vocab), BF16),
                pltpu.VMEM((per, quarter), BF16),
                pltpu.VMEM((passes, per, quarter), BF16),
                pltpu.VMEM((tokens, width), BF16),
                pltpu.VMEM((docs, docs), F32),
                pltpu.VMEM((group, share, docs), F32),
                pltpu.VMEM((ROWS, share, docs), F32),
                pltpu.VMEM((depth, share, docs), F32),
                pltpu.VMEM((docs, docs), F32),
                pltpu.VMEM((lots, tokens, columns), F32),
                pltpu.VMEM((lots, tokens, columns), BF16),
                pltpu.VMEM((lots, blocks, tokens // blocks, columns), BF16),
                pltpu.VMEM((count * length, width), BF16),
                pltpu.VMEM((picks, count), jnp.int32),
                pltpu.VMEM((1, count), F32),
                pltpu.VMEM((1, docs), jnp.int32),
                pltpu.VMEM((passage_slot.shape[0] // docs, docs), jnp.int32),
                pltpu.VMEM((vocab // 128, 128), F32),
                pltpu.VMEM((QUARTERS, owned, quarter), BF16),
                dma((7,)),
                dma((vocab // FORWARD,)),
                dma,
                dma((depth,)),
                dma((depth,)),
                dma((depth, 3)),
                dma((depth, 3)),
                dma((depth, 2)),
                dma((depth, 2)),
                dma((depth, ROWS)),
                dma((depth, ROWS)),
                dma((group,)),
                dma((group,)),
                dma((ROWS,)),
                dma((ROWS,)),
                dma((depth,)),
                dma((depth,)),
                dma((group,)),
                dma((group,)),
                dma((lots, blocks)),
                dma((lots, blocks)),
                dma((lots, blocks)),
                dma((lots, blocks)),
            ],
            compiler_params=pltpu.CompilerParams(collective_id=0, has_side_effects=True),
        )(
            hidden.reshape(count * length, width),
            positions.T,
            passage_weight.reshape(1, count),
            passage_counts.reshape(1, docs),
            passage_slot.reshape(-1, docs),
            head_weight,
            head_bias.reshape(vocab // 128, 128),
            piece,
        )
        grad, scores = pl.pallas_call(
            expand,
            out_shape=(
                jax.ShapeDtypeStruct((count * length, width), BF16),
                jax.ShapeDtypeStruct((owned, docs), F32),
            ),
            in_specs=[vmem] * 3,
            out_specs=(anywhere, vmem),
            scratch_shapes=[pltpu.VMEM((4, count * length // 4, width), BF16), dma((4,))],
        )(*(pltpu.with_memory_space_constraint(kept, pltpu.VMEM) for kept in (hits, sums, scores)))
        return scores, grad.reshape(count, length, width)

    placed = (
        P("pass", None, None),
        P("pass", None),
        P("pass"),
        P(),
        P(),
        P(None, "voc"),
        P("voc"),
        P("pass", "voc"),
    )
    return jax.shard_map(
        on_device,
        mesh=mesh,
        in_specs=placed,
        out_specs=(P("pass", None), P("pass", None, None)),
        check_vma=False,
    )
```
